256 devices in a mesh: rows: 64 (over z, x, core), segment: 2 (over y_hi), chan: 2 (over y_lo).
Axes of the slice: x: 4, y: 4 (y_hi: 2, y_lo: 2; y = y_hi * 2 + y_lo), z: 8, core: 2. Of those that a mesh axis runs over, the one named last changes fastest.
Arguments:
- features: bfloat16 [4, 64, 384, 128], P(None, 'rows', 'chan'), may hold values from -6 to 6
- caches: bfloat16 [2, 2, 2, 64, 384, 128], P('segment', None, None, 'rows', 'chan'), may hold values from -4 to 4
- conv_weights: bfloat16 [2, 2, 384, 3, 3, 3, 384], P('segment', None, 'chan'), may hold values from -0.0625 to 0.0625
- conv_bias: float32 [2, 2, 384], P('segment'), may hold values from -3 to 3
- norm_gain: float32 [2, 2, 384], P('segment'), may hold values from 0.25 to 1.75
Outputs:
- section_outputs: bfloat16 [2, 4, 64, 384, 128], P('segment', None, 'rows', 'chan')
- next_caches: bfloat16 [2, 2, 2, 64, 384, 128], P('segment', None, None, 'rows', 'chan')
The draws below stay inside these ranges and needn't reach their ends.
All inputs are finite; a program needn't handle non-finite values.
Results may differ from the reference program's by a relative error of at most 0.0057.
Values may be sent and summed in bfloat16 or wider, within the bound.
A program may use at most 64 MiB of HBM per device.

```python
import jax
import jax.numpy as jnp
from jax import lax

CHANNELS = 384
FRAMES = 4
COLS = 128
ROWS = 64
SEGMENTS = 2


def shard_levels(key, dims, split, least, top_value):
    factor_of, own = 1.0, jax.random.fold_in(key, 6)
    for dim, blocks in split:
        heights = jnp.exp(jax.random.uniform(jax.random.fold_in(own, dim), (blocks,), jnp.float32, least / len(split), top_value / len(split)))
        factor_of = factor_of * jnp.repeat(heights, dims[dim] // blocks).reshape([-1 if axis == dim else 1 for axis in range(len(dims))])
    return factor_of


def bell_draw(key, dims, scale, bound, pieces=(), dtype=jnp.bfloat16):
    values = scale * jax.random.normal(key, dims, jnp.float32)
    if pieces:
        values = values * shard_levels(key, dims, pieces, -0.22, 0.18)
    return jnp.clip(values, -bound, bound).astype(dtype)


def setup_inputs(seed: int = 0) -> dict:
    streams_of = jax.random.split(jax.random.key(seed), 6)
    features = bell_draw(streams_of[0], (FRAMES, ROWS, CHANNELS, COLS), 1.0, 6.0, ((1, 64), (2, 2)))
    caches = bell_draw(streams_of[1], (SEGMENTS, 2, 2, ROWS, CHANNELS, COLS), 0.7, 4.0, ((0, 2), (3, 64), (4, 2)))
    conv_weights = bell_draw(streams_of[2], (SEGMENTS, 2, CHANNELS, 3, 3, 3, CHANNELS), (27 * CHANNELS) ** -0.5, 0.0625, ((0, 2), (2, 2)))
    conv_bias = bell_draw(streams_of[3], (SEGMENTS, 2, CHANNELS), 0.5, 3.0, ((0, 2),), jnp.float32)
    norm_gain = jnp.clip(1.0 + 0.15 * jax.random.normal(streams_of[4], (SEGMENTS, 2, CHANNELS), jnp.float32), 0.25, 1.75)
    return {"features": features, "caches": caches, "conv_weights": conv_weights, "conv_bias": conv_bias, "norm_gain": norm_gain}


def normed_silu(source, gain):
    values = source.astype(jnp.float32)
    scale = lax.rsqrt(lax.optimization_barrier(jnp.mean(values * values, axis=2, keepdims=True)) + 1e-06)
    return jax.nn.silu(gain.astype(jnp.float32)[:, None] * values * scale).astype(jnp.bfloat16)

def causal_conv(window, kernel, offset):
    lhs = jnp.transpose(window.astype(jnp.float32), (0, 1, 3, 2))[None]
    rhs = jnp.transpose(kernel.astype(jnp.float32), (1, 2, 3, 4, 0))
    product = lax.conv_general_dilated(lhs, rhs, window_strides=(1, 1, 1), padding=((0, 0), (1, 1), (1, 1)), dimension_numbers=('NDHWC', 'DHWIO', 'NDHWC'), precision=lax.Precision.HIGHEST)[0]
    product = jnp.transpose(product, (0, 1, 3, 2))
    return product + offset.astype(jnp.float32)[:, None]

def reference(features, caches, conv_weights, conv_bias, norm_gain):
    block_input = features
    outputs = []
    cache_list = []
    for section in range(SEGMENTS):
        source = block_input
        kept = []
        for conv_index in range(2):
            activated = normed_silu(source, norm_gain[section, conv_index])
            window = jnp.concatenate([caches[section, conv_index], activated], axis=0)
            kept.append(window[-2:])
            product = causal_conv(window, conv_weights[section, conv_index], conv_bias[section, conv_index])
            if conv_index == 0:
                source = lax.optimization_barrier(product.astype(jnp.bfloat16))
            else:
                block_input = lax.optimization_barrier((block_input.astype(jnp.float32) + product).astype(jnp.bfloat16))
        outputs.append(block_input)
        cache_list.append(jnp.stack(kept))
    return (jnp.stack(outputs), jnp.stack(cache_list))
```

```python
import functools

import jax
import jax.numpy as jnp
from jax import lax
from jax.experimental import pallas as pl
from jax.experimental.pallas import tpu as pltpu
from jax.sharding import PartitionSpec as P

MESH = pl.DeviceIdType.MESH
LAG_C0, LAG_A1, LAG_C1 = 1, 2, 3


def kernel(rows, feat, cache, weights, bias, gain, out, tails, w, xa, src, acc, zbuf, bias_b, gain_b, par,
           w_sem, par_sem, half_sem, cache_sem, mid_sem, x_sem, y_send, c_send, m_send, x_send, z_send, o_sem, t_sem):
    frames, wide, cols = src.shape[1:]
    own = wide // 2
    r, s, c = lax.axis_index("rows"), lax.axis_index("segment"), lax.axis_index("chan")
    first, second = s == 0, s == 1
    mine = pl.ds(pl.multiple_of(c * own, own), own)
    theirs = pl.ds(pl.multiple_of((1 - c) * own, own), own)
    partner = (r, s, 1 - c)
    above, below = (r - 1, s, c), (r + 1, s, c)
    has_above, has_below = r > 0, r < rows - 1

    def local(source, target, sem):
        return pltpu.make_async_copy(source, target, sem)

    def remote(source, target, send, recv, device):
        return pltpu.make_async_remote_copy(
            src_ref=source, dst_ref=target, send_sem=send, recv_sem=recv, device_id=device, device_id_type=MESH
        )

    def y_feature(f):
        return remote(feat.at[f], src.at[0, f, mine], y_send.at[f], half_sem.at[f, c], partner)

    def y_cache(j, t):
        return remote(cache.at[j, t], xa.at[j, t, 1, mine], c_send.at[j, t], cache_sem.at[j, t, c], partner)

    def y_middle(f):
        return remote(src.at[1, f, mine], src.at[1, f, mine], m_send.at[f], mid_sem.at[f], partner)

    def to_below(j, t):
        return remote(xa.at[j, t, 1], xa.at[j, t, 0], x_send.at[j, t, 0], x_sem.at[j, t, 0], below)

    def to_above(j, t):
        return remote(xa.at[j, t, 1], xa.at[j, t, 2], x_send.at[j, t, 1], x_sem.at[j, t, 1], above)

    def to_next(f, side):
        return remote(zbuf.at[f], src.at[0, f, mine], z_send.at[f, side], half_sem.at[f, c], (r, 1, side))

    def own_feature(f):
        return local(feat.at[f], src.at[0, f, mine], half_sem.at[f, c])

    def own_cache(j, t):
        return local(cache.at[j, t], xa.at[j, t, 1, mine], cache_sem.at[j, t, c])

    def load_weights(j, a):
        return local(weights.at[j, a], w.at[j, a], w_sem.at[j, a])

    loads = (local(bias, par.at[0], par_sem.at[0]), local(gain, par.at[1], par_sem.at[1]))
    for load in loads:
        load.start()
    for j in range(2):
        for t in range(2):
            own_cache(j, t).start()

    @pl.when(first)
    def _():
        for f in range(frames):
            own_feature(f).start()

    barrier = pltpu.get_barrier_semaphore()

    def greet(device):
        pl.semaphore_signal(barrier, inc=1, device_id=device, device_id_type=MESH)

    greet(partner)
    greet((r, 1 - s, 0))
    greet((r, 1 - s, 1))

    @pl.when(has_above)
    def _():
        greet(above)

    @pl.when(has_below)
    def _():
        greet(below)

    pl.semaphore_wait(barrier, 3 + has_above.astype(jnp.int32) + has_below.astype(jnp.int32))

    y_cache(0, 0).start()
    y_cache(0, 1).start()

    @pl.when(first)
    def _():
        y_feature(0).start()
        y_feature(1).start()

    y_cache(1, 0).start()
    y_cache(1, 1).start()

    @pl.when(first)
    def _():
        for f in range(2, frames):
            y_feature(f).start()

    for j in range(2):
        for a in range(3):
            load_weights(j, a).start()

    @pl.when(jnp.logical_not(has_above))
    def _():
        xa[:, :, 0] = jnp.zeros_like(xa[:, :, 0])

    @pl.when(jnp.logical_not(has_below))
    def _():
        xa[:, :, 2] = jnp.zeros_like(xa[:, :, 2])

    for load in loads:
        load.wait()
    for j in range(2):
        bias_b[j] = jnp.broadcast_to(par[0, j : j + 1], (cols, wide)).T
        gain_b[j] = jnp.broadcast_to(par[1, j : j + 1], (cols, wide)).T

    def spread(j, t):
        @pl.when(has_below)
        def _():
            to_below(j, t).start()

        @pl.when(has_above)
        def _():
            to_above(j, t).start()

    def rows_arrived(j, t):
        @pl.when(has_above)
        def _():
            to_below(j, t).wait_recv()

        @pl.when(has_below)
        def _():
            to_above(j, t).wait_recv()

    def unit(j, t, a):
        total = None
        for b in range(3):
            part = jnp.dot(w[j, a, b], xa[j, t, b], preferred_element_type=jnp.float32)
            total = part if total is None else total + part
        return total

    def activate(j, f):
        if j == 0:
            for half in range(2):
                remote(zbuf.at[0], src.at[0, f, pl.ds(half * own, own)], z_send.at[f, 0], half_sem.at[f, half], partner).wait_recv()
        else:
            y_middle(f).wait_recv()
        values = src[j, f].astype(jnp.float32)
        scale = lax.rsqrt(jnp.mean(values * values, axis=0, keepdims=True) + 1e-06)
        v = gain_b[j] * values * scale
        xa[j, f + 2, 1] = (v / (1.0 + jnp.exp(-v))).astype(jnp.bfloat16)
        spread(j, f + 2)

    def spread_cache(j):
        for t in range(2):
            for half in range(2):
                remote(cache.at[j, t], xa.at[j, t, 1, pl.ds(half * own, own)], c_send.at[j, t], cache_sem.at[j, t, half], partner).wait_recv()
            spread(j, t)

    def cache_units(j):
        for a in range(2):
            load_weights(j, a).wait()
        rows_arrived(j, 0)
        acc[j, 0] = unit(j, 0, 0)
        rows_arrived(j, 1)
        acc[j, 0] += unit(j, 1, 1)
        acc[j, 1] = unit(j, 1, 0)
        load_weights(j, 2).wait()

    lane = lax.broadcasted_iota(jnp.int32, (own, cols), 1)

    def convolve(j, f):
        rows_arrived(j, f + 2)
        total = acc[j, f] + unit(j, f + 2, 2)
        left = jnp.where(lane == 0, 0.0, pltpu.roll(total[:own], 1, 1))
        right = jnp.where(lane == cols - 1, 0.0, pltpu.roll(total[2 * own :], cols - 1, 1))
        product = left + total[own : 2 * own] + right + bias_b[j, mine]
        if j == 0:
            src[1, f, mine] = product.astype(jnp.bfloat16)
            y_middle(f).start()
        else:
            zbuf[f] = (src[0, f, mine].astype(jnp.float32) + product).astype(jnp.bfloat16)

            @pl.when(first)
            def _():
                to_next(f, 0).start()
                to_next(f, 1).start()

            local(zbuf.at[f], out.at[f], o_sem.at[f]).start()

    def later_units(j, f):
        @pl.when(f < frames - 1)
        def _():
            acc[j, f + 1] += unit(j, f + 2, 1)

        @pl.when(f < frames - 2)
        def _():
            acc[j, f + 2] = unit(j, f + 2, 0)

    spread_cache(0)

    @pl.when(second)
    def _():
        spread_cache(1)
        cache_units(0)
        cache_units(1)

    def inside(f):
        return jnp.logical_and(f >= 0, f < frames)

    def slot(k, carry):
        f_c1, f_a1, f_c0, f_a0 = k - LAG_C1, k - LAG_A1, k - LAG_C0, k

        @pl.when(inside(f_c1))
        def _():
            convolve(1, f_c1)

        @pl.when(inside(f_a1))
        def _():
            activate(1, f_a1)

        @pl.when(inside(f_c0))
        def _():
            convolve(0, f_c0)

        @pl.when(inside(f_a0))
        def _():
            activate(0, f_a0)

        @pl.when(jnp.logical_and(first, k == 0))
        def _():
            cache_units(0)

        @pl.when(inside(f_c1))
        def _():
            later_units(1, f_c1)

        @pl.when(inside(f_c0))
        def _():
            later_units(0, f_c0)

        @pl.when(jnp.logical_and(first, k == 1))
        def _():
            spread_cache(1)

        @pl.when(jnp.logical_and(first, k == 2))
        def _():
            cache_units(1)

        return carry

    lax.fori_loop(0, frames + LAG_C1, slot, 0)

    def tail(j, t):
        return local(xa.at[j, frames + t, 1, mine], tails.at[j, t], t_sem.at[j, t])

    for j in range(2):
        for t in range(2):
            tail(j, t).start()
    for j in range(2):
        for t in range(2):
            tail(j, t).wait()
            y_cache(j, t).wait_send()
    for f in range(frames):
        local(zbuf.at[f], out.at[f], o_sem.at[f]).wait()
        y_middle(f).wait_send()

    @pl.when(first)
    def _():
        for f in range(frames):
            y_feature(f).wait_send()
            to_next(f, 0).wait_send()
            to_next(f, 1).wait_send()

    for j in range(2):
        for t in range(frames + 2):

            @pl.when(has_below)
            def _():
                to_below(j, t).wait_send()

            @pl.when(has_above)
            def _():
                to_above(j, t).wait_send()


def shards(rows, features, caches, conv_weights, conv_bias, norm_gain):
    frames, _, own, cols = features.shape
    wide = 2 * own
    weights = jnp.transpose(conv_weights[0], (0, 2, 3, 4, 1, 5)).reshape(2, 3, 3, 3 * own, wide)
    any_space = pl.BlockSpec(memory_space=pl.ANY)
    bf16, f32, dma = jnp.bfloat16, jnp.float32, pltpu.SemaphoreType.DMA
    out, tails = pl.pallas_call(
        functools.partial(kernel, rows),
        out_shape=(
            jax.ShapeDtypeStruct((frames, own, cols), bf16),
            jax.ShapeDtypeStruct((2, 2, own, cols), bf16),
        ),
        in_specs=[any_space] * 5,
        out_specs=(any_space, any_space),
        scratch_shapes=[
            pltpu.VMEM((2, 3, 3, 3 * own, wide), bf16),
            pltpu.VMEM((2, frames + 2, 3, wide, cols), bf16),
            pltpu.VMEM((2, frames, wide, cols), bf16),
            pltpu.VMEM((2, frames, 3 * own, cols), f32),
            pltpu.VMEM((frames, own, cols), bf16),
            pltpu.VMEM((2, wide, cols), f32),
            pltpu.VMEM((2, wide, cols), f32),
            pltpu.VMEM((2, 2, wide), f32),
            dma((2, 3)),
            dma((2,)),
            dma((frames, 2)),
            dma((2, 2, 2)),
            dma((frames,)),
            dma((2, frames + 2, 2)),
            dma((frames,)),
            dma((2, 2)),
            dma((frames,)),
            dma((2, frames + 2, 2)),
            dma((frames, 2)),
            dma((frames,)),
            dma((2, 2)),
        ],
        compiler_params=pltpu.CompilerParams(collective_id=0, has_side_effects=True, vmem_limit_bytes=48 << 20),
        name="resblocks",
    )(features[:, 0], caches[0, :, :, 0], weights, conv_bias[0], norm_gain[0])
    return (out[None, :, None], tails[None, :, :, None])


def solution(mesh):
    in_specs = (
        P(None, "rows", "chan", None),
        P("segment", None, None, "rows", "chan", None),
        P("segment", None, "chan", None, None, None, None),
        P("segment", None, None),
        P("segment", None, None),
    )
    out_specs = (
        P("segment", None, "rows", "chan", None),
        P("segment", None, None, "rows", "chan", None),
    )
    body = functools.partial(shards, mesh.shape["rows"])
    return jax.shard_map(body, mesh=mesh, in_specs=in_specs, out_specs=out_specs, check_vma=False)
```

```python
import functools

import jax
import jax.numpy as jnp
from jax import lax
from jax.experimental import pallas as pl
from jax.experimental.pallas import tpu as pltpu
from jax.sharding import PartitionSpec as P

MESH = pl.DeviceIdType.MESH
LAG_C0, LAG_A1, LAG_C1 = 2, 3, 4
RUN = 8


def kernel(rows, feat, cache, weights, bias, gain, out, tails, w, xa, src, acc, zbuf, bias_b, gain_b, par, halo,
           w_sem, par_sem, half_sem, cache_sem, mid_sem, x_sem, y_send, c_send, m_send, x_send, z_send, o_sem, t_sem,
           halo_sem, halo_cache_sem, d_send, dc_send, dz_send, cross_sem, cross_send):
    frames, wide, cols = src.shape[1:]
    own = wide // 2
    r, s, c = lax.axis_index("rows"), lax.axis_index("segment"), lax.axis_index("chan")
    first, second = s == 0, s == 1
    mine = pl.ds(pl.multiple_of(c * own, own), own)
    theirs = pl.ds(pl.multiple_of((1 - c) * own, own), own)
    partner = (r, s, 1 - c)
    above, below = (r - 1, s, c), (r + 1, s, c)
    top, bottom = r % RUN == 0, r % RUN == RUN - 1
    has_above, has_below = jnp.logical_not(top), jnp.logical_not(bottom)
    crossing = jnp.logical_or(jnp.logical_and(top, r > 0), jnp.logical_and(bottom, r < rows - 1))
    across = jnp.where(top, r - 1, r + 1)
    side = jnp.where(top, 0, 2)
    far_side = 2 - side

    def local(source, target, sem):
        return pltpu.make_async_copy(source, target, sem)

    def remote(source, target, send, recv, device):
        return pltpu.make_async_remote_copy(
            src_ref=source, dst_ref=target, send_sem=send, recv_sem=recv, device_id=device, device_id_type=MESH
        )

    def y_feature(f):
        return remote(feat.at[f], src.at[0, f, mine], y_send.at[f], half_sem.at[f, c], partner)

    def y_cache(j, t):
        return remote(cache.at[j, t], xa.at[j, t, 1, mine], c_send.at[j, t], cache_sem.at[j, t, c], partner)

    def y_middle(f):
        return remote(src.at[1, f, mine], src.at[1, f, mine], m_send.at[f], mid_sem.at[f], partner)

    def to_below(j, t):
        return remote(xa.at[j, t, 1], xa.at[j, t, 0], x_send.at[j, t, 0], x_sem.at[j, t, 0], below)

    def to_above(j, t):
        return remote(xa.at[j, t, 1], xa.at[j, t, 2], x_send.at[j, t, 1], x_sem.at[j, t, 1], above)

    def to_next(f, side):
        return remote(zbuf.at[f], src.at[0, f, mine], z_send.at[f, side], half_sem.at[f, c], (r, 1, side))

    def feature_across(to):
        return remote(feat.at[0], halo.at[0, 0, mine], d_send.at[0, 0, to], halo_sem.at[0, 0, c], (across, s, to))

    def cache_across(t, to):
        return remote(cache.at[0, t], xa.at[0, t, far_side, mine], dc_send.at[t, to], halo_cache_sem.at[t, c], (across, s, to))

    def row_across(j, t):
        return remote(xa.at[j, t, 1], xa.at[j, t, far_side], cross_send.at[j, t], cross_sem.at[j, t], (across, s, c))

    def row_from_across(j, t):
        return remote(xa.at[j, t, 1], xa.at[j, t, side], cross_send.at[j, t], cross_sem.at[j, t], (across, s, c))

    def middle_across(f, to):
        return remote(src.at[1, f, mine], halo.at[1, f, mine], d_send.at[1, f, to], halo_sem.at[1, f, c], (across, s, to))

    def next_across(to):
        return remote(zbuf.at[0], halo.at[0, 0, mine], dz_send.at[to], halo_sem.at[0, 0, c], (across, 1, to))

    def own_feature(f):
        return local(feat.at[f], src.at[0, f, mine], half_sem.at[f, c])

    def own_cache(j, t):
        return local(cache.at[j, t], xa.at[j, t, 1, mine], cache_sem.at[j, t, c])

    def load_weights(j, a):
        return local(weights.at[j, a], w.at[j, a], w_sem.at[j, a])

    barrier = pltpu.get_barrier_semaphore()

    def greet(device):
        pl.semaphore_signal(barrier, inc=1, device_id=device, device_id_type=MESH)

    greet(partner)
    for to in range(2):
        greet((r, 1 - s, to))

    @pl.when(has_above)
    def _():
        greet(above)

    @pl.when(has_below)
    def _():
        greet(below)

    @pl.when(crossing)
    def _():
        for segment in range(2):
            for to in range(2):
                greet((across, segment, to))

    loads = (local(bias, par.at[0], par_sem.at[0]), local(gain, par.at[1], par_sem.at[1]))
    for load in loads:
        load.start()
    for j in range(2):
        for t in range(2):
            own_cache(j, t).start()

    @pl.when(first)
    def _():
        for f in range(frames):
            own_feature(f).start()

    for a in range(3):
        load_weights(0, a).start()

    pl.semaphore_wait(barrier, 3 + has_above.astype(jnp.int32) + has_below.astype(jnp.int32) + 4 * crossing.astype(jnp.int32))

    def send_cache(j):
        for t in range(2):
            y_cache(j, t).start()

            if j == 0:

                @pl.when(crossing)
                def _():
                    cache_across(t, 0).start()
                    cache_across(t, 1).start()

    send_cache(0)

    @pl.when(first)
    def _():
        y_feature(0).start()

        @pl.when(crossing)
        def _():
            feature_across(0).start()
            feature_across(1).start()

        y_feature(1).start()

    @pl.when(second)
    def _():
        send_cache(1)

    for a in range(3):
        load_weights(1, a).start()

    @pl.when(r == 0)
    def _():
        xa[:, :, 0] = jnp.zeros_like(xa[:, :, 0])

    @pl.when(r == rows - 1)
    def _():
        xa[:, :, 2] = jnp.zeros_like(xa[:, :, 2])

    for load in loads:
        load.wait()
    for j in range(2):
        bias_b[j] = jnp.broadcast_to(par[0, j : j + 1], (cols, wide)).T
        gain_b[j] = jnp.broadcast_to(par[1, j : j + 1], (cols, wide)).T

    def spread(j, t):
        @pl.when(has_below)
        def _():
            to_below(j, t).start()

        @pl.when(has_above)
        def _():
            to_above(j, t).start()

    def spread_across(j, t):
        @pl.when(crossing)
        def _():
            row_across(j, t).start()

    def rows_arrived(j, t):
        @pl.when(has_above)
        def _():
            to_below(j, t).wait_recv()

        @pl.when(has_below)
        def _():
            to_above(j, t).wait_recv()

    def halo_cache_arrived(j, t):
        @pl.when(crossing)
        def _():
            if j == 0:
                for half in range(2):
                    part = pl.ds(half * own, own)
                    remote(cache.at[0, t], xa.at[0, t, side, part], dc_send.at[t, 0], halo_cache_sem.at[t, half], partner).wait_recv()
            else:
                row_from_across(j, t).wait_recv()

    def tail(j, t):
        return local(xa.at[j, frames + t, 1, mine], tails.at[j, t], t_sem.at[j, t])

    def normed(j, block):
        values = block.astype(jnp.float32)
        scale = lax.rsqrt(jnp.mean(values * values, axis=0, keepdims=True) + 1e-06)
        v = gain_b[j] * values * scale
        return (v / (1.0 + jnp.exp(-v))).astype(jnp.bfloat16)

    def halo_arrived(j, f):
        def from_halves():
            for half in range(2):
                part = pl.ds(half * own, own)
                remote(zbuf.at[f], halo.at[j, f, part], dz_send.at[0], halo_sem.at[j, f, half], partner).wait_recv()
            xa[j, f + 2, side] = normed(j, halo[j, f])

        if j == 1:
            pl.when(crossing)(from_halves)
        else:
            pl.when(jnp.logical_and(crossing, f == 0))(from_halves)

            @pl.when(jnp.logical_and(crossing, f > 0))
            def _():
                row_from_across(0, f + 2).wait_recv()

    def unit(j, t, a):
        total = None
        for b in range(3):
            part = jnp.dot(w[j, a, b], xa[j, t, b], preferred_element_type=jnp.float32)
            total = part if total is None else total + part
        return total

    def activate(j, f):
        if j == 0:
            for half in range(2):
                remote(zbuf.at[0], src.at[0, f, pl.ds(half * own, own)], z_send.at[f, 0], half_sem.at[f, half], partner).wait_recv()
        else:
            y_middle(f).wait_recv()
        xa[j, f + 2, 1] = normed(j, src[j, f])
        spread(j, f + 2)
        if j == 0:

            @pl.when(f > 0)
            def _():
                spread_across(0, f + 2)

            @pl.when(jnp.logical_and(first, f == 0))
            def _():
                y_feature(2).start()

        @pl.when(f >= frames - 2)
        def _():
            tail(j, f - (frames - 2)).start()

    def spread_cache(j):
        for t in range(2):
            for half in range(2):
                remote(cache.at[j, t], xa.at[j, t, 1, pl.ds(half * own, own)], c_send.at[j, t], cache_sem.at[j, t, half], partner).wait_recv()
            spread(j, t)
            if j == 1:
                spread_across(1, t)

    def cache_units(j):
        for a in range(2):
            load_weights(j, a).wait()
        rows_arrived(j, 0)
        halo_cache_arrived(j, 0)
        acc[j, 0] = unit(j, 0, 0)
        rows_arrived(j, 1)
        halo_cache_arrived(j, 1)
        acc[j, 0] += unit(j, 1, 1)
        acc[j, 1] = unit(j, 1, 0)
        load_weights(j, 2).wait()

    lane = lax.broadcasted_iota(jnp.int32, (own, cols), 1)

    def convolve(j, f):
        rows_arrived(j, f + 2)
        halo_arrived(j, f)
        total = acc[j, f] + unit(j, f + 2, 2)
        left = jnp.where(lane == 0, 0.0, pltpu.roll(total[:own], 1, 1))
        right = jnp.where(lane == cols - 1, 0.0, pltpu.roll(total[2 * own :], cols - 1, 1))
        product = left + total[own : 2 * own] + right + bias_b[j, mine]
        if j == 0:
            src[1, f, mine] = product.astype(jnp.bfloat16)
            y_middle(f).start()

            @pl.when(crossing)
            def _():
                middle_across(f, 0).start()
                middle_across(f, 1).start()

            @pl.when(jnp.logical_and(first, f + 3 < frames))
            def _():
                y_feature(f + 3).start()

        else:
            zbuf[f] = (src[0, f, mine].astype(jnp.float32) + product).astype(jnp.bfloat16)

            @pl.when(first)
            def _():
                to_next(f, 0).start()
                to_next(f, 1).start()

                @pl.when(jnp.logical_and(crossing, f == 0))
                def _():
                    next_across(0).start()
                    next_across(1).start()

            local(zbuf.at[f], out.at[f], o_sem.at[f]).start()

    def later_units(j, f):
        @pl.when(f < frames - 1)
        def _():
            acc[j, f + 1] += unit(j, f + 2, 1)

        @pl.when(f < frames - 2)
        def _():
            acc[j, f + 2] = unit(j, f + 2, 0)

    spread_cache(0)

    @pl.when(second)
    def _():
        spread_cache(1)
        cache_units(0)
        cache_units(1)

    def inside(f):
        return jnp.logical_and(f >= 0, f < frames)

    @pl.when(first)
    def _():
        send_cache(1)

    def slot(k, carry):
        f_c1, f_a1, f_c0, f_a0 = k - LAG_C1, k - LAG_A1, k - LAG_C0, k

        @pl.when(inside(f_c1))
        def _():
            convolve(1, f_c1)

        @pl.when(inside(f_a1))
        def _():
            activate(1, f_a1)

        @pl.when(inside(f_c0))
        def _():
            convolve(0, f_c0)

        @pl.when(inside(f_a0))
        def _():
            activate(0, f_a0)

        @pl.when(jnp.logical_and(first, k == 1))
        def _():
            cache_units(0)

        @pl.when(jnp.logical_and(first, k == 1))
        def _():
            spread_cache(1)

        @pl.when(inside(f_c1))
        def _():
            later_units(1, f_c1)

        @pl.when(inside(f_c0))
        def _():
            later_units(0, f_c0)

        @pl.when(jnp.logical_and(first, k == 3))
        def _():
            cache_units(1)

        return carry

    lax.fori_loop(0, frames + LAG_C1, slot, 0)

    for j in range(2):
        for t in range(2):
            tail(j, t).wait()
            y_cache(j, t).wait_send()
    for f in range(frames):
        local(zbuf.at[f], out.at[f], o_sem.at[f]).wait()
        y_middle(f).wait_send()

    @pl.when(first)
    def _():
        for f in range(frames):
            y_feature(f).wait_send()
            to_next(f, 0).wait_send()
            to_next(f, 1).wait_send()

    @pl.when(crossing)
    def _():
        for to in range(2):
            for t in range(2):
                cache_across(t, to).wait_send()
            for f in range(frames):
                middle_across(f, to).wait_send()
        for t in range(2):
            row_across(1, t).wait_send()
        for f in range(1, frames):
            row_across(0, f + 2).wait_send()

        @pl.when(first)
        def _():
            for to in range(2):
                feature_across(to).wait_send()
                next_across(to).wait_send()

    for j in range(2):
        for t in range(frames + 2):

            @pl.when(has_below)
            def _():
                to_below(j, t).wait_send()

            @pl.when(has_above)
            def _():
                to_above(j, t).wait_send()


def shards(rows, features, caches, conv_weights, conv_bias, norm_gain):
    frames, _, own, cols = features.shape
    wide = 2 * own
    weights = jnp.transpose(conv_weights[0], (0, 2, 3, 4, 1, 5)).reshape(2, 3, 3, 3 * own, wide)
    any_space = pl.BlockSpec(memory_space=pl.ANY)
    bf16, f32, dma = jnp.bfloat16, jnp.float32, pltpu.SemaphoreType.DMA
    out, tails = pl.pallas_call(
        functools.partial(kernel, rows),
        out_shape=(
            jax.ShapeDtypeStruct((frames, own, cols), bf16),
            jax.ShapeDtypeStruct((2, 2, own, cols), bf16),
        ),
        in_specs=[any_space] * 5,
        out_specs=(any_space, any_space),
        scratch_shapes=[
            pltpu.VMEM((2, 3, 3, 3 * own, wide), bf16),
            pltpu.VMEM((2, frames + 2, 3, wide, cols), bf16),
            pltpu.VMEM((2, frames, wide, cols), bf16),
            pltpu.VMEM((2, frames, 3 * own, cols), f32),
            pltpu.VMEM((frames, own, cols), bf16),
            pltpu.VMEM((2, wide, cols), f32),
            pltpu.VMEM((2, wide, cols), f32),
            pltpu.VMEM((2, 2, wide), f32),
            pltpu.VMEM((2, frames, wide, cols), bf16),
            dma((2, 3)),
            dma((2,)),
            dma((frames, 2)),
            dma((2, 2, 2)),
            dma((frames,)),
            dma((2, frames + 2, 2)),
            dma((frames,)),
            dma((2, 2)),
            dma((frames,)),
            dma((2, frames + 2, 2)),
            dma((frames, 2)),
            dma((frames,)),
            dma((2, 2)),
            dma((2, frames, 2)),
            dma((2, 2)),
            dma((2, frames, 2)),
            dma((2, 2)),
            dma((2,)),
            dma((2, frames + 2)),
            dma((2, frames + 2)),
        ],
        compiler_params=pltpu.CompilerParams(collective_id=0, has_side_effects=True, vmem_limit_bytes=67043328),
        name="resblocks",
    )(features[:, 0], caches[0, :, :, 0], weights, conv_bias[0], norm_gain[0])
    return (out[None, :, None], tails[None, :, :, None])


def solution(mesh):
    in_specs = (
        P(None, "rows", "chan", None),
        P("segment", None, None, "rows", "chan", None),
        P("segment", None, "chan", None, None, None, None),
        P("segment", None, None),
        P("segment", None, None),
    )
    out_specs = (
        P("segment", None, "rows", "chan", None),
        P("segment", None, None, "rows", "chan", None),
    )
    body = functools.partial(shards, mesh.shape["rows"])
    return jax.shard_map(body, mesh=mesh, in_specs=in_specs, out_specs=out_specs, check_vma=False)
```

```python
import functools

import jax
import jax.numpy as jnp
from jax import lax
from jax.experimental import pallas as pl
from jax.experimental.pallas import tpu as pltpu
from jax.sharding import PartitionSpec as P

MESH = pl.DeviceIdType.MESH
LAG_C0, LAG_A1, LAG_C1 = 2, 3, 4
RUN = 8
DIRECT = (3,)


def kernel(rows, feat, cache, weights, bias, gain, out, tails, w, xa, src, acc, zbuf, bias_b, gain_b, par, halo,
           w_sem, par_sem, half_sem, cache_sem, mid_sem, x_sem, y_send, c_send, m_send, x_send, z_send, o_sem, t_sem,
           halo_sem, halo_cache_sem, d_send, dc_send, dz_send, cross_sem, cross_send):
    frames, wide, cols = src.shape[1:]
    own = wide // 2
    r, s, c = lax.axis_index("rows"), lax.axis_index("segment"), lax.axis_index("chan")
    first, second = s == 0, s == 1
    mine = pl.ds(pl.multiple_of(c * own, own), own)
    theirs = pl.ds(pl.multiple_of((1 - c) * own, own), own)
    partner = (r, s, 1 - c)
    above, below = (r - 1, s, c), (r + 1, s, c)
    top, bottom = r % RUN == 0, r % RUN == RUN - 1
    has_above, has_below = jnp.logical_not(top), jnp.logical_not(bottom)
    crossing = jnp.logical_or(jnp.logical_and(top, r > 0), jnp.logical_and(bottom, r < rows - 1))
    across = jnp.where(top, r - 1, r + 1)
    side = jnp.where(top, 0, 2)
    far_side = 2 - side

    def local(source, target, sem):
        return pltpu.make_async_copy(source, target, sem)

    def remote(source, target, send, recv, device):
        return pltpu.make_async_remote_copy(
            src_ref=source, dst_ref=target, send_sem=send, recv_sem=recv, device_id=device, device_id_type=MESH
        )

    def y_feature(f):
        return remote(feat.at[f], src.at[0, f, mine], y_send.at[f], half_sem.at[f, c], partner)

    def y_cache(j, t):
        return remote(cache.at[j, t], xa.at[j, t, 1, mine], c_send.at[j, t], cache_sem.at[j, t, c], partner)

    def y_middle(f):
        return remote(src.at[1, f, mine], src.at[1, f, mine], m_send.at[f], mid_sem.at[f], partner)

    def to_below(j, t):
        return remote(xa.at[j, t, 1], xa.at[j, t, 0], x_send.at[j, t, 0], x_sem.at[j, t, 0], below)

    def to_above(j, t):
        return remote(xa.at[j, t, 1], xa.at[j, t, 2], x_send.at[j, t, 1], x_sem.at[j, t, 1], above)

    def to_next(f, side):
        return remote(zbuf.at[f], src.at[0, f, mine], z_send.at[f, side], half_sem.at[f, c], (r, 1, side))

    def feature_across(to):
        return remote(feat.at[0], halo.at[0, 0, mine], d_send.at[0, 0, to], halo_sem.at[0, 0, c], (across, s, to))

    def cache_across(t, to):
        return remote(cache.at[0, t], xa.at[0, t, far_side, mine], dc_send.at[t, to], halo_cache_sem.at[t, c], (across, s, to))

    def row_across(j, t):
        return remote(xa.at[j, t, 1], xa.at[j, t, far_side], cross_send.at[j, t], cross_sem.at[j, t], (across, s, c))

    def row_from_across(j, t):
        return remote(xa.at[j, t, 1], xa.at[j, t, side], cross_send.at[j, t], cross_sem.at[j, t], (across, s, c))

    def middle_across(f, to):
        return remote(src.at[1, f, mine], halo.at[1, f, mine], d_send.at[1, f, to], halo_sem.at[1, f, c], (across, s, to))

    def next_across(f, to):
        return remote(zbuf.at[f], halo.at[0, f, mine], dz_send.at[f, to], halo_sem.at[0, f, c], (across, 1, to))

    def halves_across(f):
        return jnp.logical_or(jnp.logical_and(first, f == 0), jnp.logical_and(second, sent_across(f)))

    def sent_across(f):
        return functools.reduce(jnp.logical_or, [f == one for one in DIRECT])

    def own_feature(f):
        return local(feat.at[f], src.at[0, f, mine], half_sem.at[f, c])

    def own_cache(j, t):
        return local(cache.at[j, t], xa.at[j, t, 1, mine], cache_sem.at[j, t, c])

    def load_weights(j, a):
        return local(weights.at[j, a], w.at[j, a], w_sem.at[j, a])

    barrier = pltpu.get_barrier_semaphore()

    def greet(device):
        pl.semaphore_signal(barrier, inc=1, device_id=device, device_id_type=MESH)

    greet(partner)
    for to in range(2):
        greet((r, 1 - s, to))

    @pl.when(has_above)
    def _():
        greet(above)

    @pl.when(has_below)
    def _():
        greet(below)

    @pl.when(crossing)
    def _():
        for segment in range(2):
            for to in range(2):
                greet((across, segment, to))

    loads = (local(bias, par.at[0], par_sem.at[0]), local(gain, par.at[1], par_sem.at[1]))
    for load in loads:
        load.start()
    for j in range(2):
        for t in range(2):
            own_cache(j, t).start()

    @pl.when(first)
    def _():
        for f in range(frames):
            own_feature(f).start()

    for a in range(3):
        load_weights(0, a).start()

    pl.semaphore_wait(barrier, 3 + has_above.astype(jnp.int32) + has_below.astype(jnp.int32) + 4 * crossing.astype(jnp.int32))

    def send_cache(j):
        for t in range(2):
            y_cache(j, t).start()

            if j == 0:

                @pl.when(crossing)
                def _():
                    cache_across(t, 0).start()
                    cache_across(t, 1).start()

    send_cache(0)

    @pl.when(first)
    def _():
        y_feature(0).start()

        @pl.when(crossing)
        def _():
            feature_across(0).start()
            feature_across(1).start()

        y_feature(1).start()

    @pl.when(second)
    def _():
        send_cache(1)

    for a in range(3):
        load_weights(1, a).start()

    @pl.when(r == 0)
    def _():
        xa[:, :, 0] = jnp.zeros_like(xa[:, :, 0])

    @pl.when(r == rows - 1)
    def _():
        xa[:, :, 2] = jnp.zeros_like(xa[:, :, 2])

    for load in loads:
        load.wait()
    for j in range(2):
        bias_b[j] = jnp.broadcast_to(par[0, j : j + 1], (cols, wide)).T
        gain_b[j] = jnp.broadcast_to(par[1, j : j + 1], (cols, wide)).T

    def spread(j, t):
        @pl.when(has_below)
        def _():
            to_below(j, t).start()

        @pl.when(has_above)
        def _():
            to_above(j, t).start()

    def spread_across(j, t):
        @pl.when(crossing)
        def _():
            row_across(j, t).start()

    def rows_arrived(j, t):
        @pl.when(has_above)
        def _():
            to_below(j, t).wait_recv()

        @pl.when(has_below)
        def _():
            to_above(j, t).wait_recv()

    def halo_cache_arrived(j, t):
        @pl.when(crossing)
        def _():
            if j == 0:
                for half in range(2):
                    part = pl.ds(half * own, own)
                    remote(cache.at[0, t], xa.at[0, t, side, part], dc_send.at[t, 0], halo_cache_sem.at[t, half], partner).wait_recv()
            else:
                row_from_across(j, t).wait_recv()

    def tail(j, t):
        return local(xa.at[j, frames + t, 1, mine], tails.at[j, t], t_sem.at[j, t])

    def normed(j, block):
        values = block.astype(jnp.float32)
        scale = lax.rsqrt(jnp.mean(values * values, axis=0, keepdims=True) + 1e-06)
        v = gain_b[j] * values * scale
        return (v / (1.0 + jnp.exp(-v))).astype(jnp.bfloat16)

    def halo_arrived(j, f):
        def from_halves():
            for half in range(2):
                part = pl.ds(half * own, own)
                remote(zbuf.at[f], halo.at[j, f, part], dz_send.at[f, 0], halo_sem.at[j, f, half], partner).wait_recv()
            xa[j, f + 2, side] = normed(j, halo[j, f])

        if j == 1:
            pl.when(crossing)(from_halves)
        else:
            pl.when(jnp.logical_and(crossing, halves_across(f)))(from_halves)

            @pl.when(jnp.logical_and(crossing, jnp.logical_not(halves_across(f))))
            def _():
                row_from_across(0, f + 2).wait_recv()

    def unit(j, t, a):
        total = None
        for b in range(3):
            part = jnp.dot(w[j, a, b], xa[j, t, b], preferred_element_type=jnp.float32)
            total = part if total is None else total + part
        return total

    def pair(j, t, f):
        total = None
        for b in range(3):
            both = jnp.concatenate([xa[j, t, b], xa[j, t + 1, b]], axis=1)
            part = jnp.dot(w[j, 0, b], both, preferred_element_type=jnp.float32)
            total = part if total is None else total + part
        acc[j, f] = total[:, :cols]
        acc[j, f + 1] = total[:, cols:]

    def activate(j, f):
        if j == 0:
            for half in range(2):
                remote(zbuf.at[0], src.at[0, f, pl.ds(half * own, own)], z_send.at[f, 0], half_sem.at[f, half], partner).wait_recv()
        else:
            y_middle(f).wait_recv()
        xa[j, f + 2, 1] = normed(j, src[j, f])
        spread(j, f + 2)
        if j == 0:

            @pl.when(jnp.logical_not(halves_across(f)))
            def _():
                spread_across(0, f + 2)

            @pl.when(jnp.logical_and(first, f == 0))
            def _():
                y_feature(2).start()

        @pl.when(f >= frames - 2)
        def _():
            tail(j, f - (frames - 2)).start()

    def spread_cache(j):
        for t in range(2):
            for half in range(2):
                remote(cache.at[j, t], xa.at[j, t, 1, pl.ds(half * own, own)], c_send.at[j, t], cache_sem.at[j, t, half], partner).wait_recv()
            spread(j, t)
            if j == 1:
                spread_across(1, t)

    def cache_units(j):
        for a in range(2):
            load_weights(j, a).wait()
        rows_arrived(j, 0)
        halo_cache_arrived(j, 0)
        rows_arrived(j, 1)
        halo_cache_arrived(j, 1)
        pair(j, 0, 0)
        acc[j, 0] += unit(j, 1, 1)
        load_weights(j, 2).wait()

    lane = lax.broadcasted_iota(jnp.int32, (own, cols), 1)

    def convolve(j, f):
        rows_arrived(j, f + 2)
        halo_arrived(j, f)
        total = acc[j, f] + unit(j, f + 2, 2)
        left = jnp.where(lane == 0, 0.0, pltpu.roll(total[:own], 1, 1))
        right = jnp.where(lane == cols - 1, 0.0, pltpu.roll(total[2 * own :], cols - 1, 1))
        product = left + total[own : 2 * own] + right + bias_b[j, mine]
        if j == 0:
            src[1, f, mine] = product.astype(jnp.bfloat16)
            y_middle(f).start()

            @pl.when(crossing)
            def _():
                middle_across(f, 0).start()
                middle_across(f, 1).start()

            @pl.when(jnp.logical_and(first, f + 3 < frames))
            def _():
                y_feature(f + 3).start()

        else:
            zbuf[f] = (src[0, f, mine].astype(jnp.float32) + product).astype(jnp.bfloat16)

            @pl.when(first)
            def _():
                to_next(f, 0).start()
                to_next(f, 1).start()

                @pl.when(jnp.logical_and(crossing, sent_across(f)))
                def _():
                    next_across(f, 0).start()
                    next_across(f, 1).start()

            local(zbuf.at[f], out.at[f], o_sem.at[f]).start()

    def later_units(j, f):
        @pl.when(f == 1)
        def _():
            pair(j, 2, 2)

        @pl.when(f < frames - 1)
        def _():
            acc[j, f + 1] += unit(j, f + 2, 1)

    spread_cache(0)

    @pl.when(second)
    def _():
        spread_cache(1)
        cache_units(0)
        cache_units(1)

    def inside(f):
        return jnp.logical_and(f >= 0, f < frames)

    @pl.when(first)
    def _():
        send_cache(1)

    def slot(k, carry):
        f_c1, f_a1, f_c0, f_a0 = k - LAG_C1, k - LAG_A1, k - LAG_C0, k

        @pl.when(inside(f_c0))
        def _():
            convolve(0, f_c0)

        @pl.when(inside(f_a1))
        def _():
            activate(1, f_a1)

        @pl.when(inside(f_c1))
        def _():
            convolve(1, f_c1)

        @pl.when(inside(f_a0))
        def _():
            activate(0, f_a0)

        @pl.when(jnp.logical_and(first, k == 1))
        def _():
            cache_units(0)

        @pl.when(jnp.logical_and(first, k == 1))
        def _():
            spread_cache(1)

        @pl.when(inside(f_c0))
        def _():
            later_units(0, f_c0)

        @pl.when(jnp.logical_and(first, k == 3))
        def _():
            cache_units(1)

        @pl.when(inside(f_c1))
        def _():
            later_units(1, f_c1)

        return carry

    lax.fori_loop(0, frames + LAG_C1, slot, 0)

    for j in range(2):
        for t in range(2):
            tail(j, t).wait()
            y_cache(j, t).wait_send()
    for f in range(frames):
        local(zbuf.at[f], out.at[f], o_sem.at[f]).wait()
        y_middle(f).wait_send()

    @pl.when(first)
    def _():
        for f in range(frames):
            y_feature(f).wait_send()
            to_next(f, 0).wait_send()
            to_next(f, 1).wait_send()

    @pl.when(crossing)
    def _():
        for to in range(2):
            for t in range(2):
                cache_across(t, to).wait_send()
            for f in range(frames):
                middle_across(f, to).wait_send()
        for t in range(2):
            row_across(1, t).wait_send()

        @pl.when(first)
        def _():
            for to in range(2):
                feature_across(to).wait_send()
                for f in DIRECT:
                    next_across(f, to).wait_send()
            for f in range(1, frames):
                row_across(0, f + 2).wait_send()

        @pl.when(second)
        def _():
            for f in set(range(frames)).difference(DIRECT):
                row_across(0, f + 2).wait_send()

    for j in range(2):
        for t in range(frames + 2):

            @pl.when(has_below)
            def _():
                to_below(j, t).wait_send()

            @pl.when(has_above)
            def _():
                to_above(j, t).wait_send()


def store(out, tails, out_hbm, tails_hbm, sem):
    copies = [pltpu.make_async_copy(x, y, sem.at[i]) for i, (x, y) in enumerate(((out, out_hbm), (tails, tails_hbm)))]
    for copy in copies:
        copy.start()
    for copy in copies:
        copy.wait()


def shards(rows, features, caches, conv_weights, conv_bias, norm_gain):
    frames, _, own, cols = features.shape
    wide = 2 * own
    weights = jnp.transpose(conv_weights[0], (0, 2, 3, 4, 1, 5)).reshape(2, 3, 3, 3 * own, wide)
    any_space = pl.BlockSpec(memory_space=pl.ANY)
    bf16, f32, dma = jnp.bfloat16, jnp.float32, pltpu.SemaphoreType.DMA
    out, tails = pl.pallas_call(
        functools.partial(kernel, rows),
        out_shape=(
            jax.ShapeDtypeStruct((frames, own, cols), bf16),
            jax.ShapeDtypeStruct((2, 2, own, cols), bf16),
        ),
        in_specs=[any_space] * 5,
        out_specs=(any_space, any_space),
        scratch_shapes=[
            pltpu.VMEM((2, 3, 3, 3 * own, wide), bf16),
            pltpu.VMEM((2, frames + 2, 3, wide, cols), bf16),
            pltpu.VMEM((2, frames, wide, cols), bf16),
            pltpu.VMEM((2, frames, 3 * own, cols), f32),
            pltpu.VMEM((frames, own, cols), bf16),
            pltpu.VMEM((2, wide, cols), f32),
            pltpu.VMEM((2, wide, cols), f32),
            pltpu.VMEM((2, 2, wide), f32),
            pltpu.VMEM((2, frames, wide, cols), bf16),
            dma((2, 3)),
            dma((2,)),
            dma((frames, 2)),
            dma((2, 2, 2)),
            dma((frames,)),
            dma((2, frames + 2, 2)),
            dma((frames,)),
            dma((2, 2)),
            dma((frames,)),
            dma((2, frames + 2, 2)),
            dma((frames, 2)),
            dma((frames,)),
            dma((2, 2)),
            dma((2, frames, 2)),
            dma((2, 2)),
            dma((2, frames, 2)),
            dma((2, 2)),
            dma((frames, 2)),
            dma((2, frames + 2)),
            dma((2, frames + 2)),
        ],
        compiler_params=pltpu.CompilerParams(collective_id=0, has_side_effects=True, vmem_limit_bytes=24 << 20),
        name="resblocks",
    )(*(pltpu.with_memory_space_constraint(x, pltpu.HBM) for x in (features[:, 0], caches[0, :, :, 0], weights, conv_bias[0], norm_gain[0])))
    out, tails = pl.pallas_call(
        store,
        out_shape=(jax.ShapeDtypeStruct(out.shape, bf16), jax.ShapeDtypeStruct(tails.shape, bf16)),
        in_specs=[any_space] * 2,
        out_specs=(any_space, any_space),
        scratch_shapes=[dma((2,))],
        compiler_params=pltpu.CompilerParams(vmem_limit_bytes=1 << 20),
        name="store",
    )(out, tails)
    return (out[None, :, None], tails[None, :, :, None])


def solution(mesh):
    in_specs = (
        P(None, "rows", "chan", None),
        P("segment", None, None, "rows", "chan", None),
        P("segment", None, "chan", None, None, None, None),
        P("segment", None, None),
        P("segment", None, None),
    )
    out_specs = (
        P("segment", None, "rows", "chan", None),
        P("segment", None, None, "rows", "chan", None),
    )
    body = functools.partial(shards, mesh.shape["rows"])
    return jax.shard_map(body, mesh=mesh, in_specs=in_specs, out_specs=out_specs, check_vma=False)
```

```python
import functools

import jax
import jax.numpy as jnp
from jax import lax
from jax.experimental import pallas as pl
from jax.experimental.pallas import tpu as pltpu
from jax.sharding import PartitionSpec as P

MESH = pl.DeviceIdType.MESH
LAG_C0, LAG_A1, LAG_C1 = 2, 3, 4
RUN = 8
DIRECT = (3,)


def kernel(rows, feat, cache, weights, bias, gain, out, tails, w, xa, src, acc, zbuf, bias_b, gain_b, par, halo,
           w_sem, par_sem, half_sem, cache_sem, mid_sem, x_sem, y_send, c_send, m_send, x_send, z_send, o_sem, t_sem,
           halo_sem, halo_cache_sem, d_send, dc_send, dz_send, cross_sem, cross_send):
    frames, wide, cols = src.shape[1:]
    own = wide // 2
    r, s, c = lax.axis_index("rows"), lax.axis_index("segment"), lax.axis_index("chan")
    first, second = s == 0, s == 1
    mine = pl.ds(pl.multiple_of(c * own, own), own)
    theirs = pl.ds(pl.multiple_of((1 - c) * own, own), own)
    partner = (r, s, 1 - c)
    above, below = (r - 1, s, c), (r + 1, s, c)
    top, bottom = r % RUN == 0, r % RUN == RUN - 1
    has_above, has_below = jnp.logical_not(top), jnp.logical_not(bottom)
    crossing = jnp.logical_or(jnp.logical_and(top, r > 0), jnp.logical_and(bottom, r < rows - 1))
    across = jnp.where(top, r - 1, r + 1)
    side = jnp.where(top, 0, 2)
    far_side = 2 - side

    def local(source, target, sem):
        return pltpu.make_async_copy(source, target, sem)

    def remote(source, target, send, recv, device):
        return pltpu.make_async_remote_copy(
            src_ref=source, dst_ref=target, send_sem=send, recv_sem=recv, device_id=device, device_id_type=MESH
        )

    def y_feature(f):
        return remote(feat.at[f], src.at[0, f, mine], y_send.at[f], half_sem.at[f, c], partner)

    def y_cache(j, t):
        return remote(cache.at[j, t], xa.at[j, t, 1, mine], c_send.at[j, t], cache_sem.at[j, t, c], partner)

    def y_middle(f):
        return remote(src.at[1, f, mine], src.at[1, f, mine], m_send.at[f], mid_sem.at[f], partner)

    def to_below(j, t):
        return remote(xa.at[j, t, 1], xa.at[j, t, 0], x_send.at[j, t, 0], x_sem.at[j, t, 0], below)

    def to_above(j, t):
        return remote(xa.at[j, t, 1], xa.at[j, t, 2], x_send.at[j, t, 1], x_sem.at[j, t, 1], above)

    def to_next(f, side):
        return remote(zbuf.at[f], src.at[0, f, mine], z_send.at[f, side], half_sem.at[f, c], (r, 1, side))

    def feature_across(to):
        return remote(feat.at[0], halo.at[0, 0, mine], d_send.at[0, 0, to], halo_sem.at[0, 0, c], (across, s, to))

    def cache_across(t, to):
        return remote(cache.at[0, t], xa.at[0, t, far_side, mine], dc_send.at[t, to], halo_cache_sem.at[t, c], (across, s, to))

    def row_across(j, t):
        return remote(xa.at[j, t, 1], xa.at[j, t, far_side], cross_send.at[j, t], cross_sem.at[j, t], (across, s, c))

    def row_from_across(j, t):
        return remote(xa.at[j, t, 1], xa.at[j, t, side], cross_send.at[j, t], cross_sem.at[j, t], (across, s, c))

    def middle_across(f, to):
        return remote(src.at[1, f, mine], halo.at[1, f, mine], d_send.at[1, f, to], halo_sem.at[1, f, c], (across, s, to))

    def next_across(f, to):
        return remote(zbuf.at[f], halo.at[0, f, mine], dz_send.at[f, to], halo_sem.at[0, f, c], (across, 1, to))

    def halves_across(f):
        return jnp.logical_or(jnp.logical_and(first, f == 0), jnp.logical_and(second, sent_across(f)))

    def sent_across(f):
        return functools.reduce(jnp.logical_or, [f == one for one in DIRECT])

    def own_feature(f):
        return local(feat.at[f], src.at[0, f, mine], half_sem.at[f, c])

    def own_cache(j, t):
        return local(cache.at[j, t], xa.at[j, t, 1, mine], cache_sem.at[j, t, c])

    def load_weights(j, a):
        return local(weights.at[j, a], w.at[j, a], w_sem.at[j, a])

    barrier = pltpu.get_barrier_semaphore()

    def greet(device):
        pl.semaphore_signal(barrier, inc=1, device_id=device, device_id_type=MESH)

    greet(partner)
    for to in range(2):
        greet((r, 1 - s, to))

    @pl.when(has_above)
    def _():
        greet(above)

    @pl.when(has_below)
    def _():
        greet(below)

    @pl.when(crossing)
    def _():
        for segment in range(2):
            for to in range(2):
                greet((across, segment, to))

    loads = (local(bias, par.at[0], par_sem.at[0]), local(gain, par.at[1], par_sem.at[1]))
    for load in loads:
        load.start()
    for j in range(2):
        for t in range(2):
            own_cache(j, t).start()

    @pl.when(first)
    def _():
        for f in range(frames):
            own_feature(f).start()

    for a in range(3):
        load_weights(0, a).start()

    pl.semaphore_wait(barrier, 3 + has_above.astype(jnp.int32) + has_below.astype(jnp.int32) + 4 * crossing.astype(jnp.int32))

    def send_cache(j):
        for t in range(2):
            y_cache(j, t).start()

            if j == 0:

                @pl.when(crossing)
                def _():
                    cache_across(t, 0).start()
                    cache_across(t, 1).start()

    send_cache(0)

    @pl.when(first)
    def _():
        y_feature(0).start()

        @pl.when(crossing)
        def _():
            feature_across(0).start()
            feature_across(1).start()

        y_feature(1).start()

    @pl.when(second)
    def _():
        send_cache(1)

    for a in range(3):
        load_weights(1, a).start()

    @pl.when(r == 0)
    def _():
        xa[:, :, 0] = jnp.zeros_like(xa[:, :, 0])

    @pl.when(r == rows - 1)
    def _():
        xa[:, :, 2] = jnp.zeros_like(xa[:, :, 2])

    for load in loads:
        load.wait()
    for j in range(2):
        bias_b[j] = jnp.broadcast_to(par[0, j : j + 1], (cols, wide)).T
        gain_b[j] = jnp.broadcast_to(par[1, j : j + 1], (cols, wide)).T

    def spread(j, t):
        @pl.when(has_below)
        def _():
            to_below(j, t).start()

        @pl.when(has_above)
        def _():
            to_above(j, t).start()

    def spread_across(j, t):
        @pl.when(crossing)
        def _():
            row_across(j, t).start()

    def rows_arrived(j, t):
        @pl.when(has_above)
        def _():
            to_below(j, t).wait_recv()

        @pl.when(has_below)
        def _():
            to_above(j, t).wait_recv()

    def halo_cache_arrived(j, t):
        @pl.when(crossing)
        def _():
            if j == 0:
                for half in range(2):
                    part = pl.ds(half * own, own)
                    remote(cache.at[0, t], xa.at[0, t, side, part], dc_send.at[t, 0], halo_cache_sem.at[t, half], partner).wait_recv()
            else:
                row_from_across(j, t).wait_recv()

    def tail(j, t):
        return local(xa.at[j, frames + t, 1, mine], tails.at[j, t], t_sem.at[j, t])

    def normed(j, block):
        values = block.astype(jnp.float32)
        scale = lax.rsqrt(jnp.mean(values * values, axis=0, keepdims=True) + 1e-06)
        v = gain_b[j] * values * scale
        return (v / (1.0 + jnp.exp(-v))).astype(jnp.bfloat16)

    def halo_arrived(j, f):
        def from_halves():
            for half in range(2):
                part = pl.ds(half * own, own)
                remote(zbuf.at[f], halo.at[j, f, part], dz_send.at[f, 0], halo_sem.at[j, f, half], partner).wait_recv()
            xa[j, f + 2, side] = normed(j, halo[j, f])

        if j == 1:
            pl.when(crossing)(from_halves)
        else:
            pl.when(jnp.logical_and(crossing, halves_across(f)))(from_halves)

            @pl.when(jnp.logical_and(crossing, jnp.logical_not(halves_across(f))))
            def _():
                row_from_across(0, f + 2).wait_recv()

    def unit(j, t, a):
        total = None
        for b in range(3):
            part = jnp.dot(w[j, a, b], xa[j, t, b], preferred_element_type=jnp.float32)
            total = part if total is None else total + part
        return total

    def pair(j, t, f):
        total = None
        for b in range(3):
            both = jnp.concatenate([xa[j, t, b], xa[j, t + 1, b]], axis=1)
            part = jnp.dot(w[j, 0, b], both, preferred_element_type=jnp.float32)
            total = part if total is None else total + part
        acc[j, f] = total[:, :cols]
        acc[j, f + 1] = total[:, cols:]

    def activate(j, f):
        if j == 0:
            for half in range(2):
                remote(zbuf.at[0], src.at[0, f, pl.ds(half * own, own)], z_send.at[f, 0], half_sem.at[f, half], partner).wait_recv()
        else:
            y_middle(f).wait_recv()
        xa[j, f + 2, 1] = normed(j, src[j, f])
        spread(j, f + 2)
        if j == 0:

            @pl.when(jnp.logical_not(halves_across(f)))
            def _():
                spread_across(0, f + 2)

            @pl.when(jnp.logical_and(first, f == 0))
            def _():
                y_feature(2).start()

        @pl.when(f >= frames - 2)
        def _():
            tail(j, f - (frames - 2)).start()

    def spread_cache(j):
        for t in range(2):
            for half in range(2):
                remote(cache.at[j, t], xa.at[j, t, 1, pl.ds(half * own, own)], c_send.at[j, t], cache_sem.at[j, t, half], partner).wait_recv()
            spread(j, t)
            if j == 1:
                spread_across(1, t)

    def cache_units(j):
        for a in range(2):
            load_weights(j, a).wait()
        rows_arrived(j, 0)
        halo_cache_arrived(j, 0)
        rows_arrived(j, 1)
        halo_cache_arrived(j, 1)
        pair(j, 0, 0)
        acc[j, 0] += unit(j, 1, 1)
        load_weights(j, 2).wait()

    lane = lax.broadcasted_iota(jnp.int32, (own, cols), 1)

    def convolve(j, f):
        rows_arrived(j, f + 2)
        halo_arrived(j, f)
        total = acc[j, f] + unit(j, f + 2, 2)
        left = jnp.where(lane == 0, 0.0, pltpu.roll(total[:own], 1, 1))
        right = jnp.where(lane == cols - 1, 0.0, pltpu.roll(total[2 * own :], cols - 1, 1))
        product = left + total[own : 2 * own] + right + bias_b[j, mine]
        if j == 0:
            src[1, f, mine] = product.astype(jnp.bfloat16)
            y_middle(f).start()

            @pl.when(crossing)
            def _():
                middle_across(f, 0).start()
                middle_across(f, 1).start()

            @pl.when(jnp.logical_and(first, f + 3 < frames))
            def _():
                y_feature(f + 3).start()

        else:
            zbuf[f] = (src[0, f, mine].astype(jnp.float32) + product).astype(jnp.bfloat16)

            @pl.when(first)
            def _():
                to_next(f, 0).start()
                to_next(f, 1).start()

                @pl.when(jnp.logical_and(crossing, sent_across(f)))
                def _():
                    next_across(f, 0).start()
                    next_across(f, 1).start()

            local(zbuf.at[f], out.at[f], o_sem.at[f]).start()

    def later_units(j, f):
        @pl.when(f == 1)
        def _():
            pair(j, 2, 2)

        @pl.when(f < frames - 1)
        def _():
            acc[j, f + 1] += unit(j, f + 2, 1)

    spread_cache(0)

    @pl.when(second)
    def _():
        spread_cache(1)
        cache_units(0)
        cache_units(1)

    def inside(f):
        return jnp.logical_and(f >= 0, f < frames)

    @pl.when(first)
    def _():
        send_cache(1)

    def slot(k, carry):
        f_c1, f_a1, f_c0, f_a0 = k - LAG_C1, k - LAG_A1, k - LAG_C0, k

        @pl.when(inside(f_c0))
        def _():
            convolve(0, f_c0)

        @pl.when(jnp.logical_and(first, k == 2))
        def _():
            spread_cache(1)

        @pl.when(inside(f_a1))
        def _():
            activate(1, f_a1)

        @pl.when(inside(f_c1))
        def _():
            convolve(1, f_c1)

        @pl.when(inside(f_a0))
        def _():
            activate(0, f_a0)

        @pl.when(jnp.logical_and(first, k == 1))
        def _():
            cache_units(0)

        @pl.when(inside(f_c0))
        def _():
            later_units(0, f_c0)

        @pl.when(jnp.logical_and(first, k == 3))
        def _():
            cache_units(1)

        @pl.when(inside(f_c1))
        def _():
            later_units(1, f_c1)

        return carry

    lax.fori_loop(0, frames + LAG_C1, slot, 0)

    for j in range(2):
        for t in range(2):
            tail(j, t).wait()
            y_cache(j, t).wait_send()
    for f in range(frames):
        local(zbuf.at[f], out.at[f], o_sem.at[f]).wait()
        y_middle(f).wait_send()

    @pl.when(first)
    def _():
        for f in range(frames):
            y_feature(f).wait_send()
            to_next(f, 0).wait_send()
            to_next(f, 1).wait_send()

    @pl.when(crossing)
    def _():
        for to in range(2):
            for t in range(2):
                cache_across(t, to).wait_send()
            for f in range(frames):
                middle_across(f, to).wait_send()
        for t in range(2):
            row_across(1, t).wait_send()

        @pl.when(first)
        def _():
            for to in range(2):
                feature_across(to).wait_send()
                for f in DIRECT:
                    next_across(f, to).wait_send()
            for f in range(1, frames):
                row_across(0, f + 2).wait_send()

        @pl.when(second)
        def _():
            for f in set(range(frames)).difference(DIRECT):
                row_across(0, f + 2).wait_send()

    for j in range(2):
        for t in range(frames + 2):

            @pl.when(has_below)
            def _():
                to_below(j, t).wait_send()

            @pl.when(has_above)
            def _():
                to_above(j, t).wait_send()


def store(out, tails, out_hbm, tails_hbm, sem):
    copies = [pltpu.make_async_copy(x, y, sem.at[i]) for i, (x, y) in enumerate(((out, out_hbm), (tails, tails_hbm)))]
    for copy in copies:
        copy.start()
    for copy in copies:
        copy.wait()


def shards(rows, features, caches, conv_weights, conv_bias, norm_gain):
    frames, _, own, cols = features.shape
    wide = 2 * own
    weights = jnp.transpose(conv_weights[0], (0, 2, 3, 4, 1, 5)).reshape(2, 3, 3, 3 * own, wide)
    any_space = pl.BlockSpec(memory_space=pl.ANY)
    bf16, f32, dma = jnp.bfloat16, jnp.float32, pltpu.SemaphoreType.DMA
    out, tails = pl.pallas_call(
        functools.partial(kernel, rows),
        out_shape=(
            jax.ShapeDtypeStruct((frames, own, cols), bf16),
            jax.ShapeDtypeStruct((2, 2, own, cols), bf16),
        ),
        in_specs=[any_space] * 5,
        out_specs=(any_space, any_space),
        scratch_shapes=[
            pltpu.VMEM((2, 3, 3, 3 * own, wide), bf16),
            pltpu.VMEM((2, frames + 2, 3, wide, cols), bf16),
            pltpu.VMEM((2, frames, wide, cols), bf16),
            pltpu.VMEM((2, frames, 3 * own, cols), f32),
            pltpu.VMEM((frames, own, cols), bf16),
            pltpu.VMEM((2, wide, cols), f32),
            pltpu.VMEM((2, wide, cols), f32),
            pltpu.VMEM((2, 2, wide), f32),
            pltpu.VMEM((2, frames, wide, cols), bf16),
            dma((2, 3)),
            dma((2,)),
            dma((frames, 2)),
            dma((2, 2, 2)),
            dma((frames,)),
            dma((2, frames + 2, 2)),
            dma((frames,)),
            dma((2, 2)),
            dma((frames,)),
            dma((2, frames + 2, 2)),
            dma((frames, 2)),
            dma((frames,)),
            dma((2, 2)),
            dma((2, frames, 2)),
            dma((2, 2)),
            dma((2, frames, 2)),
            dma((2, 2)),
            dma((frames, 2)),
            dma((2, frames + 2)),
            dma((2, frames + 2)),
        ],
        compiler_params=pltpu.CompilerParams(collective_id=0, has_side_effects=True, vmem_limit_bytes=24 << 20),
        name="resblocks",
    )(*(pltpu.with_memory_space_constraint(x, pltpu.HBM) for x in (features[:, 0], caches[0, :, :, 0], weights, conv_bias[0], norm_gain[0])))
    out, tails = pl.pallas_call(
        store,
        out_shape=(jax.ShapeDtypeStruct(out.shape, bf16), jax.ShapeDtypeStruct(tails.shape, bf16)),
        in_specs=[any_space] * 2,
        out_specs=(any_space, any_space),
        scratch_shapes=[dma((2,))],
        compiler_params=pltpu.CompilerParams(vmem_limit_bytes=1 << 20),
        name="store",
    )(out, tails)
    return (out[None, :, None], tails[None, :, :, None])


def solution(mesh):
    in_specs = (
        P(None, "rows", "chan", None),
        P("segment", None, None, "rows", "chan", None),
        P("segment", None, "chan", None, None, None, None),
        P("segment", None, None),
        P("segment", None, None),
    )
    out_specs = (
        P("segment", None, "rows", "chan", None),
        P("segment", None, None, "rows", "chan", None),
    )
    body = functools.partial(shards, mesh.shape["rows"])
    return jax.shard_map(body, mesh=mesh, in_specs=in_specs, out_specs=out_specs, check_vma=False)
```

```python
import functools

import jax
import jax.numpy as jnp
from jax import lax
from jax.experimental import pallas as pl
from jax.experimental.pallas import tpu as pltpu
from jax.sharding import PartitionSpec as P

MESH = pl.DeviceIdType.MESH
LAG_C0, LAG_A1, LAG_C1 = 2, 3, 4
RUN = 8
DIRECT = (3,)


def kernel(rows, feat, cache, weights, bias, gain, out, tails, w, xa, src, acc, zbuf, bias_b, gain_b, par, halo,
           w_sem, par_sem, half_sem, cache_sem, mid_sem, x_sem, y_send, c_send, m_send, x_send, z_send, o_sem, t_sem,
           halo_sem, halo_cache_sem, d_send, dc_send, dz_send, cross_sem, cross_send):
    frames, wide, cols = src.shape[1:]
    own = wide // 2
    r, s, c = lax.axis_index("rows"), lax.axis_index("segment"), lax.axis_index("chan")
    first, second = s == 0, s == 1
    mine = pl.ds(pl.multiple_of(c * own, own), own)
    theirs = pl.ds(pl.multiple_of((1 - c) * own, own), own)
    partner = (r, s, 1 - c)
    above, below = (r - 1, s, c), (r + 1, s, c)
    top, bottom = r % RUN == 0, r % RUN == RUN - 1
    has_above, has_below = jnp.logical_not(top), jnp.logical_not(bottom)
    crossing = jnp.logical_or(jnp.logical_and(top, r > 0), jnp.logical_and(bottom, r < rows - 1))
    across = jnp.where(top, r - 1, r + 1)
    side = jnp.where(top, 0, 2)
    far_side = 2 - side

    def local(source, target, sem):
        return pltpu.make_async_copy(source, target, sem)

    def take(ref, sem):
        local(ref, ref, sem).wait()

    def remote(source, target, send, recv, device):
        return pltpu.make_async_remote_copy(
            src_ref=source, dst_ref=target, send_sem=send, recv_sem=recv, device_id=device, device_id_type=MESH
        )

    def y_feature(f):
        return remote(feat.at[f], src.at[0, f, mine], y_send, half_sem.at[f], partner)

    def y_cache(j, t):
        return remote(cache.at[j, t], xa.at[j, t, 1, mine], c_send, cache_sem.at[j, t], partner)

    def y_middle(f):
        return remote(src.at[1, f, mine], src.at[1, f, mine], m_send, mid_sem.at[f], partner)

    def to_below(j, t):
        return remote(xa.at[j, t, 1], xa.at[j, t, 0], x_send.at[0], x_sem.at[j, t], below)

    def to_above(j, t):
        return remote(xa.at[j, t, 1], xa.at[j, t, 2], x_send.at[1], x_sem.at[j, t], above)

    def to_next(f, side):
        return remote(zbuf.at[f], src.at[0, f, mine], z_send.at[side], half_sem.at[f], (r, 1, side))

    def feature_across(to):
        return remote(feat.at[0], halo.at[0, 0, mine], d_send.at[0, to], halo_sem.at[0, 0], (across, s, to))

    def cache_across(t, to):
        return remote(cache.at[0, t], xa.at[0, t, far_side, mine], dc_send.at[to], halo_cache_sem.at[t], (across, s, to))

    def row_across(j, t):
        return remote(xa.at[j, t, 1], xa.at[j, t, far_side], cross_send.at[j], cross_sem.at[j, t], (across, s, c))

    def row_from_across(j, t):
        return remote(xa.at[j, t, 1], xa.at[j, t, side], cross_send.at[j], cross_sem.at[j, t], (across, s, c))

    def middle_across(f, to):
        return remote(src.at[1, f, mine], halo.at[1, f, mine], d_send.at[1, to], halo_sem.at[1, f], (across, s, to))

    def next_across(f, to):
        return remote(zbuf.at[f], halo.at[0, f, mine], dz_send.at[to], halo_sem.at[0, f], (across, 1, to))

    def halves_across(f):
        return jnp.logical_or(jnp.logical_and(first, f == 0), jnp.logical_and(second, sent_across(f)))

    def sent_across(f):
        return functools.reduce(jnp.logical_or, [f == one for one in DIRECT])

    def own_feature(f):
        return local(feat.at[f], src.at[0, f, mine], half_sem.at[f])

    def own_cache(j, t):
        return local(cache.at[j, t], xa.at[j, t, 1, mine], cache_sem.at[j, t])

    def load_weights(j, a):
        return local(weights.at[j, a], w.at[j, a], w_sem.at[j])

    barrier = pltpu.get_barrier_semaphore()

    def greet(device):
        pl.semaphore_signal(barrier, inc=1, device_id=device, device_id_type=MESH)

    greet(partner)
    for to in range(2):
        greet((r, 1 - s, to))

    @pl.when(has_above)
    def _():
        greet(above)

    @pl.when(has_below)
    def _():
        greet(below)

    @pl.when(crossing)
    def _():
        for segment in range(2):
            for to in range(2):
                greet((across, segment, to))

    loads = (local(bias, par.at[0], par_sem), local(gain, par.at[1], par_sem))
    for load in loads:
        load.start()
    for j in range(2):
        for t in range(2):
            own_cache(j, t).start()

    @pl.when(first)
    def _():
        for f in range(frames):
            own_feature(f).start()

    for a in range(3):
        load_weights(0, a).start()

    pl.semaphore_wait(barrier, 3 + has_above.astype(jnp.int32) + has_below.astype(jnp.int32) + 4 * crossing.astype(jnp.int32))

    def send_cache(j):
        for t in range(2):
            y_cache(j, t).start()

            if j == 0:

                @pl.when(crossing)
                def _():
                    cache_across(t, 0).start()
                    cache_across(t, 1).start()

    send_cache(0)

    @pl.when(first)
    def _():
        y_feature(0).start()

        @pl.when(crossing)
        def _():
            feature_across(0).start()
            feature_across(1).start()

        y_feature(1).start()

    @pl.when(second)
    def _():
        send_cache(1)

    for a in range(3):
        load_weights(1, a).start()

    @pl.when(r == 0)
    def _():
        xa[:, :, 0] = jnp.zeros_like(xa[:, :, 0])

    @pl.when(r == rows - 1)
    def _():
        xa[:, :, 2] = jnp.zeros_like(xa[:, :, 2])

    take(par, par_sem)
    for j in range(2):
        bias_b[j] = jnp.broadcast_to(par[0, j : j + 1], (cols, wide)).T
        gain_b[j] = jnp.broadcast_to(par[1, j : j + 1], (cols, wide)).T

    def spread(j, t):
        @pl.when(has_below)
        def _():
            to_below(j, t).start()

        @pl.when(has_above)
        def _():
            to_above(j, t).start()

    def spread_across(j, t):
        @pl.when(crossing)
        def _():
            row_across(j, t).start()

    def rows_arrived(j, t):
        both = jnp.logical_and(has_above, has_below)

        @pl.when(both)
        def _():
            take(xa.at[j, t, pl.ds(0, 2)], x_sem.at[j, t])

        @pl.when(jnp.logical_not(both))
        def _():
            take(xa.at[j, t, 0], x_sem.at[j, t])

    def halo_cache_arrived(j, t):
        @pl.when(crossing)
        def _():
            if j == 0:
                take(xa.at[0, t, side], halo_cache_sem.at[t])
            else:
                row_from_across(j, t).wait_recv()

    def tail(j, t):
        return local(xa.at[j, frames + t, 1, mine], tails.at[j, t], t_sem)

    def normed(j, block):
        values = block.astype(jnp.float32)
        scale = lax.rsqrt(jnp.mean(values * values, axis=0, keepdims=True) + 1e-06)
        v = gain_b[j] * values * scale
        return (v / (1.0 + jnp.exp(-v))).astype(jnp.bfloat16)

    def halo_arrived(j, f):
        def from_halves():
            take(halo.at[j, f], halo_sem.at[j, f])
            xa[j, f + 2, side] = normed(j, halo[j, f])

        if j == 1:
            pl.when(crossing)(from_halves)
        else:
            pl.when(jnp.logical_and(crossing, halves_across(f)))(from_halves)

            @pl.when(jnp.logical_and(crossing, jnp.logical_not(halves_across(f))))
            def _():
                row_from_across(0, f + 2).wait_recv()

    def unit(j, t, a):
        total = None
        for b in range(3):
            part = jnp.dot(w[j, a, b], xa[j, t, b], preferred_element_type=jnp.float32)
            total = part if total is None else total + part
        return total

    def pair(j, t, f):
        total = None
        for b in range(3):
            both = jnp.concatenate([xa[j, t, b], xa[j, t + 1, b]], axis=1)
            part = jnp.dot(w[j, 0, b], both, preferred_element_type=jnp.float32)
            total = part if total is None else total + part
        acc[j, f] = total[:, :cols]
        acc[j, f + 1] = total[:, cols:]

    def activate(j, f):
        if j == 0:
            take(src.at[0, f], half_sem.at[f])
        else:
            y_middle(f).wait_recv()
        xa[j, f + 2, 1] = normed(j, src[j, f])
        spread(j, f + 2)
        if j == 0:

            @pl.when(jnp.logical_not(halves_across(f)))
            def _():
                spread_across(0, f + 2)

            @pl.when(jnp.logical_and(first, f == 0))
            def _():
                y_feature(2).start()

        @pl.when(f >= frames - 2)
        def _():
            tail(j, f - (frames - 2)).start()

    def spread_cache(j):
        for t in range(2):
            take(xa.at[j, t, 1], cache_sem.at[j, t])
            spread(j, t)
            if j == 1:
                spread_across(1, t)

    def cache_units(j):
        take(w.at[j], w_sem.at[j])
        rows_arrived(j, 0)
        halo_cache_arrived(j, 0)
        rows_arrived(j, 1)
        halo_cache_arrived(j, 1)
        pair(j, 0, 0)
        acc[j, 0] += unit(j, 1, 1)

    lane = lax.broadcasted_iota(jnp.int32, (own, cols), 1)

    def convolve(j, f):
        halo_arrived(j, f)
        rows_arrived(j, f + 2)
        total = acc[j, f] + unit(j, f + 2, 2)
        left = jnp.where(lane == 0, 0.0, pltpu.roll(total[:own], 1, 1))
        right = jnp.where(lane == cols - 1, 0.0, pltpu.roll(total[2 * own :], cols - 1, 1))
        product = left + total[own : 2 * own] + right + bias_b[j, mine]
        if j == 0:
            src[1, f, mine] = product.astype(jnp.bfloat16)
            y_middle(f).start()

            @pl.when(crossing)
            def _():
                middle_across(f, 0).start()
                middle_across(f, 1).start()

            @pl.when(jnp.logical_and(first, f + 3 < frames))
            def _():
                y_feature(f + 3).start()

        else:
            zbuf[f] = (src[0, f, mine].astype(jnp.float32) + product).astype(jnp.bfloat16)

            @pl.when(first)
            def _():
                to_next(f, 0).start()
                to_next(f, 1).start()

                @pl.when(jnp.logical_and(crossing, sent_across(f)))
                def _():
                    next_across(f, 0).start()
                    next_across(f, 1).start()

            local(zbuf.at[f], out.at[f], o_sem).start()

    def later_units(j, f):
        @pl.when(f == 1)
        def _():
            pair(j, 2, 2)

        @pl.when(f < frames - 1)
        def _():
            acc[j, f + 1] += unit(j, f + 2, 1)

    spread_cache(0)

    @pl.when(second)
    def _():
        spread_cache(1)
        cache_units(0)
        cache_units(1)

    def inside(f):
        return jnp.logical_and(f >= 0, f < frames)

    @pl.when(first)
    def _():
        send_cache(1)

    def slot(k, carry):
        f_c1, f_a1, f_c0, f_a0 = k - LAG_C1, k - LAG_A1, k - LAG_C0, k

        @pl.when(inside(f_c0))
        def _():
            convolve(0, f_c0)

        @pl.when(jnp.logical_and(first, k == 2))
        def _():
            spread_cache(1)

        @pl.when(inside(f_a1))
        def _():
            activate(1, f_a1)

        @pl.when(inside(f_c1))
        def _():
            convolve(1, f_c1)

        @pl.when(inside(f_a0))
        def _():
            activate(0, f_a0)

        @pl.when(jnp.logical_and(first, k == 1))
        def _():
            cache_units(0)

        @pl.when(inside(f_c0))
        def _():
            later_units(0, f_c0)

        @pl.when(jnp.logical_and(first, k == 3))
        def _():
            cache_units(1)

        @pl.when(inside(f_c1))
        def _():
            later_units(1, f_c1)

        return carry

    lax.fori_loop(0, frames + LAG_C1, slot, 0)

    take(tails, t_sem)
    take(zbuf, o_sem)
    take(cache, c_send)
    take(src.at[1, :, mine], m_send)

    @pl.when(first)
    def _():
        take(feat, y_send)
        for to in range(2):
            take(zbuf, z_send.at[to])

    @pl.when(crossing)
    def _():
        for to in range(2):
            take(cache.at[0], dc_send.at[to])
            take(src.at[1, :, mine], d_send.at[1, to])
        for t, j in ((2, 1), (frames - 1, 0)):
            take(xa.at[j, pl.ds(0, t), 1], cross_send.at[j])

        @pl.when(first)
        def _():
            for to in range(2):
                take(feat.at[0], d_send.at[0, to])
                take(zbuf.at[pl.ds(0, len(DIRECT))], dz_send.at[to])

    @pl.when(has_below)
    def _():
        take(xa.at[:, :, 1], x_send.at[0])

    @pl.when(has_above)
    def _():
        take(xa.at[:, :, 1], x_send.at[1])


def store(out, tails, out_hbm, tails_hbm, sem):
    copies = [pltpu.make_async_copy(x, y, sem.at[i]) for i, (x, y) in enumerate(((out, out_hbm), (tails, tails_hbm)))]
    for copy in copies:
        copy.start()
    for copy in copies:
        copy.wait()


def shards(rows, features, caches, conv_weights, conv_bias, norm_gain):
    frames, _, own, cols = features.shape
    wide = 2 * own
    weights = jnp.transpose(conv_weights[0], (0, 2, 3, 4, 1, 5)).reshape(2, 3, 3, 3 * own, wide)
    any_space = pl.BlockSpec(memory_space=pl.ANY)
    bf16, f32, dma = jnp.bfloat16, jnp.float32, pltpu.SemaphoreType.DMA
    out, tails = pl.pallas_call(
        functools.partial(kernel, rows),
        out_shape=(
            jax.ShapeDtypeStruct((frames, own, cols), bf16),
            jax.ShapeDtypeStruct((2, 2, own, cols), bf16),
        ),
        in_specs=[any_space] * 5,
        out_specs=(any_space, any_space),
        scratch_shapes=[
            pltpu.VMEM((2, 3, 3, 3 * own, wide), bf16),
            pltpu.VMEM((2, frames + 2, 3, wide, cols), bf16),
            pltpu.VMEM((2, frames, wide, cols), bf16),
            pltpu.VMEM((2, frames, 3 * own, cols), f32),
            pltpu.VMEM((frames, own, cols), bf16),
            pltpu.VMEM((2, wide, cols), f32),
            pltpu.VMEM((2, wide, cols), f32),
            pltpu.VMEM((2, 2, wide), f32),
            pltpu.VMEM((2, frames, wide, cols), bf16),
            dma((2,)),
            dma(()),
            dma((frames,)),
            dma((2, 2)),
            dma((frames,)),
            dma((2, frames + 2)),
            dma(()),
            dma(()),
            dma(()),
            dma((2,)),
            dma((2,)),
            dma(()),
            dma(()),
            dma((2, frames)),
            dma((2,)),
            dma((2, 2)),
            dma((2,)),
            dma((2,)),
            dma((2, frames + 2)),
            dma((2,)),
        ],
        compiler_params=pltpu.CompilerParams(collective_id=0, has_side_effects=True, vmem_limit_bytes=24 << 20),
        name="resblocks",
    )(*(pltpu.with_memory_space_constraint(x, pltpu.HBM) for x in (features[:, 0], caches[0, :, :, 0], weights, conv_bias[0], norm_gain[0])))
    out, tails = pl.pallas_call(
        store,
        out_shape=(jax.ShapeDtypeStruct(out.shape, bf16), jax.ShapeDtypeStruct(tails.shape, bf16)),
        in_specs=[any_space] * 2,
        out_specs=(any_space, any_space),
        scratch_shapes=[dma((2,))],
        compiler_params=pltpu.CompilerParams(vmem_limit_bytes=1 << 20),
        name="store",
    )(out, tails)
    return (out[None, :, None], tails[None, :, :, None])


def solution(mesh):
    in_specs = (
        P(None, "rows", "chan", None),
        P("segment", None, None, "rows", "chan", None),
        P("segment", None, "chan", None, None, None, None),
        P("segment", None, None),
        P("segment", None, None),
    )
    out_specs = (
        P("segment", None, "rows", "chan", None),
        P("segment", None, None, "rows", "chan", None),
    )
    body = functools.partial(shards, mesh.shape["rows"])
    return jax.shard_map(body, mesh=mesh, in_specs=in_specs, out_specs=out_specs, check_vma=False)
```

```python
import functools

import jax
import jax.numpy as jnp
from jax import lax
from jax.experimental import pallas as pl
from jax.experimental.pallas import tpu as pltpu
from jax.sharding import PartitionSpec as P

MESH = pl.DeviceIdType.MESH
LAG_C0, LAG_A1, LAG_C1 = 2, 3, 4
RUN = 8
DIRECT = (3,)


def kernel(rows, feat, cache, weights, bias, gain, out, tails, w, xa, src, acc, zbuf, bias_b, gain_b, par, halo,
           w_sem, par_sem, half_sem, cache_sem, mid_sem, x_sem, y_send, c_send, m_send, x_send, z_send, o_sem, t_sem,
           halo_sem, halo_cache_sem, d_send, dc_send, dz_send, cross_sem, cross_send):
    frames, wide, cols = src.shape[1:]
    own = wide // 2
    r, s, c = lax.axis_index("rows"), lax.axis_index("segment"), lax.axis_index("chan")
    first, second = s == 0, s == 1
    mine = pl.ds(pl.multiple_of(c * own, own), own)
    theirs = pl.ds(pl.multiple_of((1 - c) * own, own), own)
    partner = (r, s, 1 - c)
    above, below = (r - 1, s, c), (r + 1, s, c)
    top, bottom = r % RUN == 0, r % RUN == RUN - 1
    has_above, has_below = jnp.logical_not(top), jnp.logical_not(bottom)
    crossing = jnp.logical_or(jnp.logical_and(top, r > 0), jnp.logical_and(bottom, r < rows - 1))
    across = jnp.where(top, r - 1, r + 1)
    side = jnp.where(top, 0, 2)
    far_side = 2 - side

    def local(source, target, sem):
        return pltpu.make_async_copy(source, target, sem)

    def take(ref, sem):
        local(ref, ref, sem).wait()

    def remote(source, target, send, recv, device):
        return pltpu.make_async_remote_copy(
            src_ref=source, dst_ref=target, send_sem=send, recv_sem=recv, device_id=device, device_id_type=MESH
        )

    def y_feature(f):
        return remote(feat.at[f], src.at[0, f, mine], y_send, half_sem.at[f], partner)

    def y_cache(j, t):
        return remote(cache.at[j, t], xa.at[j, t, 1, mine], c_send, cache_sem.at[j, t], partner)

    def y_middle(f):
        return remote(src.at[1, f, mine], src.at[1, f, mine], m_send, mid_sem.at[f], partner)

    def to_below(j, t):
        return remote(xa.at[j, t, 1], xa.at[j, t, 0], x_send.at[0], x_sem.at[j, t], below)

    def to_above(j, t):
        return remote(xa.at[j, t, 1], xa.at[j, t, 2], x_send.at[1], x_sem.at[j, t], above)

    def to_next(f, side):
        return remote(zbuf.at[f], src.at[0, f, mine], z_send.at[side], half_sem.at[f], (r, 1, side))

    def feature_across(to):
        return remote(feat.at[0], halo.at[0, 0, mine], d_send.at[0, to], halo_sem.at[0, 0], (across, s, to))

    def cache_across(t, to):
        return remote(cache.at[0, t], xa.at[0, t, far_side, mine], dc_send.at[to], halo_cache_sem.at[t], (across, s, to))

    def row_across(j, t):
        return remote(xa.at[j, t, 1], xa.at[j, t, far_side], cross_send.at[j], cross_sem.at[j, t], (across, s, c))

    def row_from_across(j, t):
        return remote(xa.at[j, t, 1], xa.at[j, t, side], cross_send.at[j], cross_sem.at[j, t], (across, s, c))

    def middle_across(f, to):
        return remote(src.at[1, f, mine], halo.at[1, f, mine], d_send.at[1, to], halo_sem.at[1, f], (across, s, to))

    def next_across(f, to):
        return remote(zbuf.at[f], halo.at[0, f, mine], dz_send.at[to], halo_sem.at[0, f], (across, 1, to))

    def halves_across(f):
        return jnp.logical_or(jnp.logical_and(first, f == 0), jnp.logical_and(second, sent_across(f)))

    def sent_across(f):
        return functools.reduce(jnp.logical_or, [f == one for one in DIRECT])

    def own_feature(f):
        return local(feat.at[f], src.at[0, f, mine], half_sem.at[f])

    def own_cache(j, t):
        return local(cache.at[j, t], xa.at[j, t, 1, mine], cache_sem.at[j, t])

    def load_weights(j, a):
        return local(weights.at[j, a], w.at[j, a], w_sem.at[j])

    barrier = pltpu.get_barrier_semaphore()

    def greet(device):
        pl.semaphore_signal(barrier, inc=1, device_id=device, device_id_type=MESH)

    greet(partner)
    for to in range(2):
        greet((r, 1 - s, to))

    @pl.when(has_above)
    def _():
        greet(above)

    @pl.when(has_below)
    def _():
        greet(below)

    @pl.when(crossing)
    def _():
        for segment in range(2):
            for to in range(2):
                greet((across, segment, to))

    loads = (local(bias, par.at[0], par_sem), local(gain, par.at[1], par_sem))
    for load in loads:
        load.start()
    for j in range(2):
        for t in range(2):
            own_cache(j, t).start()

    @pl.when(first)
    def _():
        for f in range(frames):
            own_feature(f).start()

    for a in range(3):
        load_weights(0, a).start()

    pl.semaphore_wait(barrier, 3 + has_above.astype(jnp.int32) + has_below.astype(jnp.int32) + 4 * crossing.astype(jnp.int32))

    def send_cache(j):
        for t in range(2):
            y_cache(j, t).start()

            if j == 0:

                @pl.when(crossing)
                def _():
                    cache_across(t, 0).start()
                    cache_across(t, 1).start()

    send_cache(0)

    @pl.when(first)
    def _():
        y_feature(0).start()

        @pl.when(crossing)
        def _():
            feature_across(0).start()
            feature_across(1).start()

        y_feature(1).start()

    @pl.when(second)
    def _():
        send_cache(1)

    for a in range(3):
        load_weights(1, a).start()

    @pl.when(r == 0)
    def _():
        xa[:, :, 0] = jnp.zeros_like(xa[:, :, 0])

    @pl.when(r == rows - 1)
    def _():
        xa[:, :, 2] = jnp.zeros_like(xa[:, :, 2])

    take(par, par_sem)
    for j in range(2):
        bias_b[j] = jnp.broadcast_to(par[0, j : j + 1], (cols, wide)).T
        gain_b[j] = jnp.broadcast_to(par[1, j : j + 1], (cols, wide)).T

    def spread(j, t):
        @pl.when(has_below)
        def _():
            to_below(j, t).start()

        @pl.when(has_above)
        def _():
            to_above(j, t).start()

    def spread_across(j, t):
        @pl.when(crossing)
        def _():
            row_across(j, t).start()

    def rows_arrived(j, t):
        both = jnp.logical_and(has_above, has_below)

        @pl.when(both)
        def _():
            take(xa.at[j, t, pl.ds(0, 2)], x_sem.at[j, t])

        @pl.when(jnp.logical_not(both))
        def _():
            take(xa.at[j, t, 0], x_sem.at[j, t])

    def halo_cache_arrived(j, t):
        @pl.when(crossing)
        def _():
            if j == 0:
                take(xa.at[0, t, side], halo_cache_sem.at[t])
            else:
                row_from_across(j, t).wait_recv()

    def tail(j, t):
        return local(xa.at[j, frames + t, 1, mine], tails.at[j, t], t_sem)

    def normed(j, block):
        values = block.astype(jnp.float32)
        scale = lax.rsqrt(jnp.mean(values * values, axis=0, keepdims=True) + 1e-06)
        v = gain_b[j] * values * scale
        return (v / (1.0 + jnp.exp(-v))).astype(jnp.bfloat16)

    def halo_arrived(j, f):
        def from_halves():
            take(halo.at[j, f], halo_sem.at[j, f])
            xa[j, f + 2, side] = normed(j, halo[j, f])

        if j == 1:
            pl.when(crossing)(from_halves)
        else:
            pl.when(jnp.logical_and(crossing, halves_across(f)))(from_halves)

            @pl.when(jnp.logical_and(crossing, jnp.logical_not(halves_across(f))))
            def _():
                row_from_across(0, f + 2).wait_recv()

    def unit(j, t, a):
        total = None
        for b in range(3):
            part = jnp.dot(w[j, a, b], xa[j, t, b], preferred_element_type=jnp.float32)
            total = part if total is None else total + part
        return total

    def pair(j, t, f):
        total = None
        for b in range(3):
            both = jnp.concatenate([xa[j, t, b], xa[j, t + 1, b]], axis=1)
            part = jnp.dot(w[j, 0, b], both, preferred_element_type=jnp.float32)
            total = part if total is None else total + part
        acc[j, f] = total[:, :cols]
        acc[j, f + 1] = total[:, cols:]

    def activate(j, f):
        if j == 0:
            take(src.at[0, f], half_sem.at[f])
        else:
            y_middle(f).wait_recv()
        xa[j, f + 2, 1] = normed(j, src[j, f])
        spread(j, f + 2)
        if j == 0:

            @pl.when(jnp.logical_not(halves_across(f)))
            def _():
                spread_across(0, f + 2)

            @pl.when(jnp.logical_and(first, f == 0))
            def _():
                y_feature(2).start()

        @pl.when(f >= frames - 2)
        def _():
            tail(j, f - (frames - 2)).start()

    def spread_cache(j):
        for t in range(2):
            take(xa.at[j, t, 1], cache_sem.at[j, t])
            spread(j, t)
            if j == 1:
                spread_across(1, t)

    def cache_units(j):
        take(w.at[j], w_sem.at[j])
        rows_arrived(j, 0)
        halo_cache_arrived(j, 0)
        rows_arrived(j, 1)
        halo_cache_arrived(j, 1)
        pair(j, 0, 0)
        acc[j, 0] += unit(j, 1, 1)

    lane = lax.broadcasted_iota(jnp.int32, (own, cols), 1)

    def convolve(j, f):
        halo_arrived(j, f)
        rows_arrived(j, f + 2)
        total = acc[j, f] + unit(j, f + 2, 2)
        left = jnp.where(lane == 0, 0.0, pltpu.roll(total[:own], 1, 1))
        right = jnp.where(lane == cols - 1, 0.0, pltpu.roll(total[2 * own :], cols - 1, 1))
        product = left + total[own : 2 * own] + right + bias_b[j, mine]
        if j == 0:
            src[1, f, mine] = product.astype(jnp.bfloat16)
            y_middle(f).start()

            @pl.when(crossing)
            def _():
                middle_across(f, 0).start()
                middle_across(f, 1).start()

            @pl.when(jnp.logical_and(first, f + 3 < frames))
            def _():
                y_feature(f + 3).start()

        else:
            zbuf[f] = (src[0, f, mine].astype(jnp.float32) + product).astype(jnp.bfloat16)

            @pl.when(first)
            def _():
                to_next(f, 0).start()
                to_next(f, 1).start()

                @pl.when(jnp.logical_and(crossing, sent_across(f)))
                def _():
                    next_across(f, 0).start()
                    next_across(f, 1).start()

            local(zbuf.at[f], out.at[f], o_sem).start()

    def later_units(j, f):
        @pl.when(f == 1)
        def _():
            pair(j, 2, 2)

        @pl.when(f < frames - 1)
        def _():
            acc[j, f + 1] += unit(j, f + 2, 1)

    spread_cache(0)

    @pl.when(second)
    def _():
        spread_cache(1)
        cache_units(0)
        cache_units(1)

    def inside(f):
        return jnp.logical_and(f >= 0, f < frames)

    @pl.when(first)
    def _():
        send_cache(1)

    def slot(k, carry):
        f_c1, f_a1, f_c0, f_a0 = k - LAG_C1, k - LAG_A1, k - LAG_C0, k

        @pl.when(inside(f_c0))
        def _():
            convolve(0, f_c0)

        @pl.when(jnp.logical_and(first, k == 2))
        def _():
            spread_cache(1)

        @pl.when(inside(f_a1))
        def _():
            activate(1, f_a1)

        @pl.when(inside(f_c1))
        def _():
            convolve(1, f_c1)

        @pl.when(jnp.logical_and(first, k == 1))
        def _():
            cache_units(0)

        @pl.when(inside(f_a0))
        def _():
            activate(0, f_a0)

        @pl.when(inside(f_c0))
        def _():
            later_units(0, f_c0)

        @pl.when(jnp.logical_and(first, k == 3))
        def _():
            cache_units(1)

        @pl.when(inside(f_c1))
        def _():
            later_units(1, f_c1)

        return carry

    lax.fori_loop(0, frames + LAG_C1, slot, 0)

    take(tails, t_sem)
    take(zbuf, o_sem)
    take(cache, c_send)
    take(src.at[1, :, mine], m_send)

    @pl.when(first)
    def _():
        take(feat, y_send)
        for to in range(2):
            take(zbuf, z_send.at[to])

    @pl.when(crossing)
    def _():
        for to in range(2):
            take(cache.at[0], dc_send.at[to])
            take(src.at[1, :, mine], d_send.at[1, to])
        for t, j in ((2, 1), (frames - 1, 0)):
            take(xa.at[j, pl.ds(0, t), 1], cross_send.at[j])

        @pl.when(first)
        def _():
            for to in range(2):
                take(feat.at[0], d_send.at[0, to])
                take(zbuf.at[pl.ds(0, len(DIRECT))], dz_send.at[to])

    @pl.when(has_below)
    def _():
        take(xa.at[:, :, 1], x_send.at[0])

    @pl.when(has_above)
    def _():
        take(xa.at[:, :, 1], x_send.at[1])


def store(out, tails, out_hbm, tails_hbm, sem):
    copies = [pltpu.make_async_copy(x, y, sem.at[i]) for i, (x, y) in enumerate(((out, out_hbm), (tails, tails_hbm)))]
    for copy in copies:
        copy.start()
    for copy in copies:
        copy.wait()


def shards(rows, features, caches, conv_weights, conv_bias, norm_gain):
    frames, _, own, cols = features.shape
    wide = 2 * own
    weights = jnp.transpose(conv_weights[0], (0, 2, 3, 4, 1, 5)).reshape(2, 3, 3, 3 * own, wide)
    any_space = pl.BlockSpec(memory_space=pl.ANY)
    bf16, f32, dma = jnp.bfloat16, jnp.float32, pltpu.SemaphoreType.DMA
    out, tails = pl.pallas_call(
        functools.partial(kernel, rows),
        out_shape=(
            jax.ShapeDtypeStruct((frames, own, cols), bf16),
            jax.ShapeDtypeStruct((2, 2, own, cols), bf16),
        ),
        in_specs=[any_space] * 5,
        out_specs=(any_space, any_space),
        scratch_shapes=[
            pltpu.VMEM((2, 3, 3, 3 * own, wide), bf16),
            pltpu.VMEM((2, frames + 2, 3, wide, cols), bf16),
            pltpu.VMEM((2, frames, wide, cols), bf16),
            pltpu.VMEM((2, frames, 3 * own, cols), f32),
            pltpu.VMEM((frames, own, cols), bf16),
            pltpu.VMEM((2, wide, cols), f32),
            pltpu.VMEM((2, wide, cols), f32),
            pltpu.VMEM((2, 2, wide), f32),
            pltpu.VMEM((2, frames, wide, cols), bf16),
            dma((2,)),
            dma(()),
            dma((frames,)),
            dma((2, 2)),
            dma((frames,)),
            dma((2, frames + 2)),
            dma(()),
            dma(()),
            dma(()),
            dma((2,)),
            dma((2,)),
            dma(()),
            dma(()),
            dma((2, frames)),
            dma((2,)),
            dma((2, 2)),
            dma((2,)),
            dma((2,)),
            dma((2, frames + 2)),
            dma((2,)),
        ],
        compiler_params=pltpu.CompilerParams(collective_id=0, has_side_effects=True, vmem_limit_bytes=24 << 20),
        name="resblocks",
    )(*(pltpu.with_memory_space_constraint(x, pltpu.HBM) for x in (features[:, 0], caches[0, :, :, 0], weights, conv_bias[0], norm_gain[0])))
    out, tails = pl.pallas_call(
        store,
        out_shape=(jax.ShapeDtypeStruct(out.shape, bf16), jax.ShapeDtypeStruct(tails.shape, bf16)),
        in_specs=[any_space] * 2,
        out_specs=(any_space, any_space),
        scratch_shapes=[dma((2,))],
        compiler_params=pltpu.CompilerParams(vmem_limit_bytes=1 << 20),
        name="store",
    )(out, tails)
    return (out[None, :, None], tails[None, :, :, None])


def solution(mesh):
    in_specs = (
        P(None, "rows", "chan", None),
        P("segment", None, None, "rows", "chan", None),
        P("segment", None, "chan", None, None, None, None),
        P("segment", None, None),
        P("segment", None, None),
    )
    out_specs = (
        P("segment", None, "rows", "chan", None),
        P("segment", None, None, "rows", "chan", None),
    )
    body = functools.partial(shards, mesh.shape["rows"])
    return jax.shard_map(body, mesh=mesh, in_specs=in_specs, out_specs=out_specs, check_vma=False)
```

```python
import functools

import jax
import jax.numpy as jnp
from jax import lax
from jax.experimental import pallas as pl
from jax.experimental.pallas import tpu as pltpu
from jax.sharding import PartitionSpec as P

MESH = pl.DeviceIdType.MESH
LAG_C0, LAG_A1, LAG_C1 = 2, 3, 4
RUN = 8
DIRECT = (3,)


def kernel(rows, feat, cache, weights, bias, gain, out, tails, w, xa, src, acc, zbuf, bias_b, gain_b, par, halo,
           w_sem, par_sem, half_sem, cache_sem, mid_sem, x_sem, y_send, c_send, m_send, x_send, z_send, o_sem, t_sem,
           halo_sem, halo_cache_sem, d_send, dc_send, dz_send, cross_sem, cross_send, ready):
    frames, wide, cols = src.shape[1:]
    own = wide // 2
    r, s, c = lax.axis_index("rows"), lax.axis_index("segment"), lax.axis_index("chan")
    first, second = s == 0, s == 1
    mine = pl.ds(pl.multiple_of(c * own, own), own)
    theirs = pl.ds(pl.multiple_of((1 - c) * own, own), own)
    partner = (r, s, 1 - c)
    above, below = (r - 1, s, c), (r + 1, s, c)
    top, bottom = r % RUN == 0, r % RUN == RUN - 1
    has_above, has_below = jnp.logical_not(top), jnp.logical_not(bottom)
    crossing = jnp.logical_or(jnp.logical_and(top, r > 0), jnp.logical_and(bottom, r < rows - 1))
    across = jnp.where(top, r - 1, r + 1)
    side = jnp.where(top, 0, 2)
    far_side = 2 - side

    def local(source, target, sem):
        return pltpu.make_async_copy(source, target, sem)

    def take(ref, sem):
        local(ref, ref, sem).wait()

    def remote(source, target, send, recv, device):
        return pltpu.make_async_remote_copy(
            src_ref=source, dst_ref=target, send_sem=send, recv_sem=recv, device_id=device, device_id_type=MESH
        )

    def y_feature(f):
        return remote(feat.at[f], src.at[0, f, mine], y_send, half_sem.at[f], partner)

    def y_cache(j, t):
        return remote(cache.at[j, t], xa.at[j, t, 1, mine], c_send, cache_sem.at[j, t], partner)

    def y_middle(f):
        return remote(src.at[1, f, mine], src.at[1, f, mine], m_send, mid_sem.at[f], partner)

    def to_below(j, t):
        return remote(xa.at[j, t, 1], xa.at[j, t, 0], x_send.at[0], x_sem.at[j, t], below)

    def to_above(j, t):
        return remote(xa.at[j, t, 1], xa.at[j, t, 2], x_send.at[1], x_sem.at[j, t], above)

    def to_next(f, side):
        return remote(zbuf.at[f], src.at[0, f, mine], z_send.at[side], half_sem.at[f], (r, 1, side))

    def feature_across(to):
        return remote(feat.at[0], halo.at[0, 0, mine], d_send.at[0, to], halo_sem.at[0, 0], (across, s, to))

    def cache_across(t, to):
        return remote(cache.at[0, t], xa.at[0, t, far_side, mine], dc_send.at[to], halo_cache_sem.at[t], (across, s, to))

    def row_across(j, t):
        return remote(xa.at[j, t, 1], xa.at[j, t, far_side], cross_send.at[j], cross_sem.at[j, t], (across, s, c))

    def row_from_across(j, t):
        return remote(xa.at[j, t, 1], xa.at[j, t, side], cross_send.at[j], cross_sem.at[j, t], (across, s, c))

    def middle_across(f, to):
        return remote(src.at[1, f, mine], halo.at[1, f, mine], d_send.at[1, to], halo_sem.at[1, f], (across, s, to))

    def next_across(f, to):
        return remote(zbuf.at[f], halo.at[0, f, mine], dz_send.at[to], halo_sem.at[0, f], (across, 1, to))

    def halves_across(f):
        return jnp.logical_or(jnp.logical_and(first, f == 0), jnp.logical_and(second, sent_across(f)))

    def sent_across(f):
        return functools.reduce(jnp.logical_or, [f == one for one in DIRECT])

    def own_feature(f):
        return local(feat.at[f], src.at[0, f, mine], half_sem.at[f])

    def own_cache(j, t):
        return local(cache.at[j, t], xa.at[j, t, 1, mine], cache_sem.at[j, t])

    def load_weights(j, a):
        return local(weights.at[j, a], w.at[j, a], w_sem.at[j])

    barrier = pltpu.get_barrier_semaphore()

    def greet(device):
        pl.semaphore_signal(barrier, inc=1, device_id=device, device_id_type=MESH)

    greet(partner)
    for to in range(2):
        greet((r, 1 - s, to))

    @pl.when(has_above)
    def _():
        greet(above)

    @pl.when(has_below)
    def _():
        greet(below)

    @pl.when(crossing)
    def _():
        for to in range(2):
            greet((across, s, to))

    loads = (local(bias, par.at[0], par_sem), local(gain, par.at[1], par_sem))
    for load in loads:
        load.start()
    for j in range(2):
        for t in range(2):
            own_cache(j, t).start()

    @pl.when(first)
    def _():
        for f in range(frames):
            own_feature(f).start()

    for a in range(3):
        load_weights(0, a).start()

    pl.semaphore_wait(barrier, 3 + has_above.astype(jnp.int32) + has_below.astype(jnp.int32) + 2 * crossing.astype(jnp.int32))

    def send_cache(j):
        for t in range(2):
            y_cache(j, t).start()

            if j == 0:

                @pl.when(crossing)
                def _():
                    cache_across(t, 0).start()
                    cache_across(t, 1).start()

    send_cache(0)

    @pl.when(first)
    def _():
        y_feature(0).start()

        @pl.when(crossing)
        def _():
            feature_across(0).start()
            feature_across(1).start()

        y_feature(1).start()

    @pl.when(second)
    def _():
        send_cache(1)

    for a in range(3):
        load_weights(1, a).start()

    @pl.when(r == 0)
    def _():
        xa[:, :, 0] = jnp.zeros_like(xa[:, :, 0])

    @pl.when(r == rows - 1)
    def _():
        xa[:, :, 2] = jnp.zeros_like(xa[:, :, 2])

    take(par, par_sem)
    for j in range(2):
        bias_b[j] = jnp.broadcast_to(par[0, j : j + 1], (cols, wide)).T
        gain_b[j] = jnp.broadcast_to(par[1, j : j + 1], (cols, wide)).T

    def spread(j, t):
        @pl.when(has_below)
        def _():
            to_below(j, t).start()

        @pl.when(has_above)
        def _():
            to_above(j, t).start()

    def spread_across(j, t):
        @pl.when(crossing)
        def _():
            row_across(j, t).start()

    def rows_arrived(j, t):
        both = jnp.logical_and(has_above, has_below)

        @pl.when(both)
        def _():
            take(xa.at[j, t, pl.ds(0, 2)], x_sem.at[j, t])

        @pl.when(jnp.logical_not(both))
        def _():
            take(xa.at[j, t, 0], x_sem.at[j, t])

    def halo_cache_arrived(j, t):
        @pl.when(crossing)
        def _():
            if j == 0:
                take(xa.at[0, t, side], halo_cache_sem.at[t])
            else:
                row_from_across(j, t).wait_recv()

    def tail(j, t):
        return local(xa.at[j, frames + t, 1, mine], tails.at[j, t], t_sem)

    def normed(j, block):
        values = block.astype(jnp.float32)
        scale = lax.rsqrt(jnp.mean(values * values, axis=0, keepdims=True) + 1e-06)
        v = gain_b[j] * values * scale
        return (v / (1.0 + jnp.exp(-v))).astype(jnp.bfloat16)

    def halo_arrived(j, f):
        def from_halves():
            take(halo.at[j, f], halo_sem.at[j, f])
            xa[j, f + 2, side] = normed(j, halo[j, f])

        if j == 1:
            pl.when(crossing)(from_halves)
        else:
            pl.when(jnp.logical_and(crossing, halves_across(f)))(from_halves)

            @pl.when(jnp.logical_and(crossing, jnp.logical_not(halves_across(f))))
            def _():
                row_from_across(0, f + 2).wait_recv()

    def unit(j, t, a):
        total = None
        for b in range(3):
            part = jnp.dot(w[j, a, b], xa[j, t, b], preferred_element_type=jnp.float32)
            total = part if total is None else total + part
        return total

    def pair(j, t, f):
        total = None
        for b in range(3):
            both = jnp.concatenate([xa[j, t, b], xa[j, t + 1, b]], axis=1)
            part = jnp.dot(w[j, 0, b], both, preferred_element_type=jnp.float32)
            total = part if total is None else total + part
        acc[j, f] = total[:, :cols]
        acc[j, f + 1] = total[:, cols:]

    def activate(j, f):
        if j == 0:
            take(src.at[0, f], half_sem.at[f])
        else:
            y_middle(f).wait_recv()
        xa[j, f + 2, 1] = normed(j, src[j, f])
        spread(j, f + 2)
        if j == 0:

            @pl.when(jnp.logical_not(halves_across(f)))
            def _():
                spread_across(0, f + 2)

            @pl.when(jnp.logical_and(first, f == 0))
            def _():
                y_feature(2).start()

        @pl.when(f >= frames - 2)
        def _():
            tail(j, f - (frames - 2)).start()

    def spread_cache(j):
        for t in range(2):
            take(xa.at[j, t, 1], cache_sem.at[j, t])
            spread(j, t)
            if j == 1:
                spread_across(1, t)

    def cache_units(j):
        take(w.at[j], w_sem.at[j])
        rows_arrived(j, 0)
        halo_cache_arrived(j, 0)
        rows_arrived(j, 1)
        halo_cache_arrived(j, 1)
        pair(j, 0, 0)
        acc[j, 0] += unit(j, 1, 1)

    lane = lax.broadcasted_iota(jnp.int32, (own, cols), 1)

    def convolve(j, f):
        halo_arrived(j, f)
        rows_arrived(j, f + 2)
        total = acc[j, f] + unit(j, f + 2, 2)
        left = jnp.where(lane == 0, 0.0, pltpu.roll(total[:own], 1, 1))
        right = jnp.where(lane == cols - 1, 0.0, pltpu.roll(total[2 * own :], cols - 1, 1))
        product = left + total[own : 2 * own] + right + bias_b[j, mine]
        if j == 0:
            src[1, f, mine] = product.astype(jnp.bfloat16)
            y_middle(f).start()

            @pl.when(crossing)
            def _():
                middle_across(f, 0).start()
                middle_across(f, 1).start()

            @pl.when(jnp.logical_and(first, f + 3 < frames))
            def _():
                y_feature(f + 3).start()

        else:
            zbuf[f] = (src[0, f, mine].astype(jnp.float32) + product).astype(jnp.bfloat16)

            @pl.when(first)
            def _():
                to_next(f, 0).start()
                to_next(f, 1).start()

                @pl.when(jnp.logical_and(crossing, sent_across(f)))
                def _():
                    pl.semaphore_wait(ready, 2)
                    next_across(f, 0).start()
                    next_across(f, 1).start()

            local(zbuf.at[f], out.at[f], o_sem).start()

    def later_units(j, f):
        @pl.when(f == 1)
        def _():
            pair(j, 2, 2)

        @pl.when(f < frames - 1)
        def _():
            acc[j, f + 1] += unit(j, f + 2, 1)

    spread_cache(0)

    @pl.when(second)
    def _():
        spread_cache(1)
        cache_units(0)
        cache_units(1)

    def inside(f):
        return jnp.logical_and(f >= 0, f < frames)

    @pl.when(first)
    def _():
        send_cache(1)

    def slot(k, carry):
        f_c1, f_a1, f_c0, f_a0 = k - LAG_C1, k - LAG_A1, k - LAG_C0, k

        @pl.when(inside(f_c0))
        def _():
            convolve(0, f_c0)

        @pl.when(jnp.logical_and(first, k == 2))
        def _():
            spread_cache(1)

        @pl.when(inside(f_a1))
        def _():
            activate(1, f_a1)

        @pl.when(inside(f_c1))
        def _():
            convolve(1, f_c1)

        @pl.when(jnp.logical_and(first, k == 1))
        def _():
            cache_units(0)

        @pl.when(inside(f_a0))
        def _():
            activate(0, f_a0)

        @pl.when(jnp.logical_and(k == 0, jnp.logical_and(second, crossing)))
        def _():
            for to in range(2):
                pl.semaphore_signal(ready, inc=1, device_id=(across, 0, to), device_id_type=MESH)

        @pl.when(inside(f_c0))
        def _():
            later_units(0, f_c0)

        @pl.when(jnp.logical_and(first, k == 3))
        def _():
            cache_units(1)

        @pl.when(inside(f_c1))
        def _():
            later_units(1, f_c1)

        return carry

    lax.fori_loop(0, frames + LAG_C1, slot, 0)

    take(tails, t_sem)
    take(zbuf, o_sem)
    take(cache, c_send)
    take(src.at[1, :, mine], m_send)

    @pl.when(first)
    def _():
        take(feat, y_send)
        for to in range(2):
            take(zbuf, z_send.at[to])

    @pl.when(crossing)
    def _():
        for to in range(2):
            take(cache.at[0], dc_send.at[to])
            take(src.at[1, :, mine], d_send.at[1, to])
        for t, j in ((2, 1), (frames - 1, 0)):
            take(xa.at[j, pl.ds(0, t), 1], cross_send.at[j])

        @pl.when(first)
        def _():
            for to in range(2):
                take(feat.at[0], d_send.at[0, to])
                take(zbuf.at[pl.ds(0, len(DIRECT))], dz_send.at[to])

    @pl.when(has_below)
    def _():
        take(xa.at[:, :, 1], x_send.at[0])

    @pl.when(has_above)
    def _():
        take(xa.at[:, :, 1], x_send.at[1])


def store(out, tails, out_hbm, tails_hbm, sem):
    copies = [pltpu.make_async_copy(x, y, sem.at[i]) for i, (x, y) in enumerate(((out, out_hbm), (tails, tails_hbm)))]
    for copy in copies:
        copy.start()
    for copy in copies:
        copy.wait()


def shards(rows, features, caches, conv_weights, conv_bias, norm_gain):
    frames, _, own, cols = features.shape
    wide = 2 * own
    weights = jnp.transpose(conv_weights[0], (0, 2, 3, 4, 1, 5)).reshape(2, 3, 3, 3 * own, wide)
    any_space = pl.BlockSpec(memory_space=pl.ANY)
    bf16, f32, dma = jnp.bfloat16, jnp.float32, pltpu.SemaphoreType.DMA
    out, tails = pl.pallas_call(
        functools.partial(kernel, rows),
        out_shape=(
            jax.ShapeDtypeStruct((frames, own, cols), bf16),
            jax.ShapeDtypeStruct((2, 2, own, cols), bf16),
        ),
        in_specs=[any_space] * 5,
        out_specs=(any_space, any_space),
        scratch_shapes=[
            pltpu.VMEM((2, 3, 3, 3 * own, wide), bf16),
            pltpu.VMEM((2, frames + 2, 3, wide, cols), bf16),
            pltpu.VMEM((2, frames, wide, cols), bf16),
            pltpu.VMEM((2, frames, 3 * own, cols), f32),
            pltpu.VMEM((frames, own, cols), bf16),
            pltpu.VMEM((2, wide, cols), f32),
            pltpu.VMEM((2, wide, cols), f32),
            pltpu.VMEM((2, 2, wide), f32),
            pltpu.VMEM((2, frames, wide, cols), bf16),
            dma((2,)),
            dma(()),
            dma((frames,)),
            dma((2, 2)),
            dma((frames,)),
            dma((2, frames + 2)),
            dma(()),
            dma(()),
            dma(()),
            dma((2,)),
            dma((2,)),
            dma(()),
            dma(()),
            dma((2, frames)),
            dma((2,)),
            dma((2, 2)),
            dma((2,)),
            dma((2,)),
            dma((2, frames + 2)),
            dma((2,)),
            pltpu.SemaphoreType.REGULAR,
        ],
        compiler_params=pltpu.CompilerParams(collective_id=0, has_side_effects=True, vmem_limit_bytes=24 << 20),
        name="resblocks",
    )(*(pltpu.with_memory_space_constraint(x, pltpu.HBM) for x in (features[:, 0], caches[0, :, :, 0], weights, conv_bias[0], norm_gain[0])))
    out, tails = pl.pallas_call(
        store,
        out_shape=(jax.ShapeDtypeStruct(out.shape, bf16), jax.ShapeDtypeStruct(tails.shape, bf16)),
        in_specs=[any_space] * 2,
        out_specs=(any_space, any_space),
        scratch_shapes=[dma((2,))],
        compiler_params=pltpu.CompilerParams(vmem_limit_bytes=1 << 20),
        name="store",
    )(out, tails)
    return (out[None, :, None], tails[None, :, :, None])


def solution(mesh):
    in_specs = (
        P(None, "rows", "chan", None),
        P("segment", None, None, "rows", "chan", None),
        P("segment", None, "chan", None, None, None, None),
        P("segment", None, None),
        P("segment", None, None),
    )
    out_specs = (
        P("segment", None, "rows", "chan", None),
        P("segment", None, None, "rows", "chan", None),
    )
    body = functools.partial(shards, mesh.shape["rows"])
    return jax.shard_map(body, mesh=mesh, in_specs=in_specs, out_specs=out_specs, check_vma=False)
```
